32 devices in a mesh: tm: 4 (over y, core), expert: 8 (over z, x).
Axes of the slice: x: 2, y: 2, z: 4, core: 2. Of those that a mesh axis runs over, the one named last changes fastest.
Arguments:
- states: bfloat16 [4, 1024, 2048], P('tm', 'expert'), may hold values from -6 to 6
- terminal: float32 [1024, 2048], P('expert'), may hold values from -6 to 6
- gates: float32 [4, 1024, 2], P('tm', 'expert'), may hold values from 0.25 to 1
- routes: int32 [4, 1024, 2], P('tm', 'expert'), may hold values from 0 to 7, all different within a row; in each aligned block of 32 rows (0 to 31, 32 to 63, ..., all dimensions but the last counted through in order) at most 12 rows name the same one
- w_in: bfloat16 [8, 2048, 2048], P('expert'), may hold values from -0.125 to 0.125
- w_out: bfloat16 [8, 2048, 2048], P('expert'), may hold values from -0.125 to 0.125
Outputs:
- adjoints: float32 [4, 1024, 2048], P('tm', 'expert')
The draws below stay inside these ranges and needn't reach their ends.
Inputs may be any that keep to these rules, and one draw needn't show every extreme that they name: `routes`: the 2 experts of a token at a step differ. In each aligned block of 32 rows of one step (one micro-batch of one device), no expert is named by more than 12 rows, a bound that some block reaches.
All inputs are finite; a program needn't handle non-finite values.
Results may differ from the reference program's by a relative error of at most 0.006.
Values may be sent and summed in bfloat16 or wider, within the bound.
A program may use at most 64 MiB of HBM per device.

```python
import math
import jax
import jax.numpy as jnp
import numpy as np
from jax import lax

D = 2048
FF = 2048
TOP = 2
MB = 32
TOKENS = 1024
EXPERTS = 8
NSTEP = 4
CAP = 12


def shard_levels(rng, extent, split, least, top_value):
    def one(axis_at, shards_of):
        heights = jax.random.uniform(jax.random.fold_in(jax.random.fold_in(rng, 6), axis_at), (shards_of,), jnp.float32, least / len(split), top_value / len(split))
        return jnp.repeat(jnp.exp(heights), extent[axis_at] // shards_of).reshape((-1,) + (1,) * (len(extent) - axis_at - 1))

    loudness = one(*split[0])
    for cut in split[1:]:
        loudness = loudness * one(*cut)
    return loudness


def deal_out(own_key, own, number, rows, count, top, reach, skew):
    ranking = jax.random.permutation(own_key, count)
    heavy_load, ordinary = load_shares(count, rows * top, reach, skew, True), load_shares(count, rows * top, reach, skew, False)
    places = jnp.arange(count)

    def named(sizes, turn):
        used = int((sizes > 0).sum())
        fixed = max(1, used // 4)
        passed = fixed + (places - fixed + turn * (used - fixed)) % max(1, count - fixed)
        return jnp.zeros((count,), jnp.int32).at[ranking[jnp.where(places < fixed, places, passed)]].set(jnp.asarray(sizes, jnp.int32))

    sizes = jnp.where(number % 4 == 0, named(heavy_load, number // 4), named(ordinary, number - number // 4 - 1))
    mixed = jax.random.permutation(jax.random.fold_in(own, 3), count)
    source_of, receiver = mixed[0:count // 2 * 2:2], mixed[1:count // 2 * 2:2]
    slack = jnp.minimum(sizes[source_of] - 1, reach - sizes[receiver]) // 2
    slack = jnp.where((source_of == ranking[0]) | (receiver == ranking[0]) | (sizes[receiver] == 0), 0, jnp.maximum(slack, 0))
    passed = jax.random.randint(jax.random.fold_in(own, 4), (count // 2,), 0, 1 << 20) % (slack + 1)
    sizes = sizes.at[source_of].add(-passed).at[receiver].add(passed)
    members = jnp.searchsorted(jnp.cumsum(sizes), jnp.arange(rows * top), side="right").astype(jnp.int32)
    table = members.reshape(top, rows).T
    table = table[jax.random.permutation(jax.random.fold_in(own, 1), rows)]
    turn = jax.random.randint(jax.random.fold_in(own, 2), (rows, 1), 0, top)
    return jnp.take_along_axis(table, (jnp.arange(top)[None, :] + turn) % top, axis=1)


def load_shares(count, total, reach, lean, full):
    loads = [(1 << 20) // math.isqrt(rank ** lean) + 1 for rank in range(1, count + 1)]
    largest = reach if full else min(reach, max(-(-total // count), total * loads[0] // sum(loads)))
    least = 1 if total - largest >= count - 1 else 0
    counts, rest = [largest] + [least] * (count - 1), total - largest - least * (count - 1)
    while rest > 0:
        free = [i for i in range(1, count) if counts[i] < largest] or [i for i in range(1, count) if counts[i] < reach]
        whole, remaining = sum([loads[i] for i in free]), rest
        for i in free:
            more = min(reach - counts[i], max(1, remaining * loads[i] // whole), rest)
            counts[i] = counts[i] + more
            rest = rest - more
    return np.array(counts)


def scatter_about(key, extent, deviation, most, pieces=(), kind=jnp.bfloat16):
    array = jax.random.normal(key, extent, jnp.float32) * deviation
    if len(pieces) > 0:
        array = shard_levels(key, extent, pieces, -0.22, 0.18) * array
    return jnp.clip(array, min=-most, max=most).astype(kind)


def setup_inputs(seed: int = 0) -> dict:
    arg_keys = jax.random.split(jax.random.key(seed), 7)
    states = scatter_about(arg_keys[0], (NSTEP, TOKENS, D), 1.0, 6.0, ((0, 4), (1, 8)))
    terminal = scatter_about(arg_keys[1], (TOKENS, D), 1.0, 6.0, ((0, 8),), jnp.float32)
    gates = jnp.clip(0.25 + 0.75 * jax.random.uniform(arg_keys[2], (NSTEP, TOKENS, TOP), jnp.float32) ** shard_levels(arg_keys[2], (NSTEP, TOKENS, TOP), ((0, 4), (1, 8)), -0.2, 0.2), 0.25, 1.0)
    routes_keys = jax.random.split(jax.random.fold_in(arg_keys[3], 1), NSTEP * TOKENS // MB)
    routes_turns = jax.random.permutation(jax.random.fold_in(arg_keys[3], 3), NSTEP * TOKENS // MB)
    routes = jax.vmap(lambda own, number: deal_out(jax.random.fold_in(arg_keys[3], 2), own, number, MB, EXPERTS, TOP, CAP, 2))(routes_keys, routes_turns).reshape((NSTEP, TOKENS, TOP))
    w_in = scatter_about(arg_keys[4], (EXPERTS, D, FF), D ** -0.5, 0.125, ((0, 8),))
    w_out = scatter_about(arg_keys[5], (EXPERTS, FF, D), FF ** -0.5, 0.125, ((0, 8),))
    return dict(states=states, terminal=terminal, gates=gates, routes=routes, w_in=w_in, w_out=w_out)


step_size = 0.5


def gelu_slope(preact):
    inside = 0.7978845608 * (preact + 0.044715 * preact ** 3)
    tangent = jnp.tanh(inside)
    return 0.5 * (1.0 + tangent) + 0.5 * preact * (1.0 - tangent * tangent) * 0.7978845608 * (1.0 + 3.0 * 0.044715 * preact * preact)


def reference(states, terminal, gates, routes, w_in, w_out):
    expert_count = w_in.shape[0]
    tokens = states.shape[1]
    width = states.shape[2]
    blocks = tokens // MB
    token_ids = jnp.arange(tokens, dtype=jnp.int32)
    owner_ids = jnp.repeat(token_ids, TOP)

    def one_step(adjoint, inputs):
        layer_in, step_gates, step_routes = inputs
        flattened = step_routes.reshape(blocks, MB * TOP)
        onehot = (flattened[:, :, None] == jnp.arange(expert_count, dtype=jnp.int32)[None, None, :]).astype(jnp.int32)
        running = jnp.cumsum(onehot, axis=1)
        slot = jnp.sum(onehot * running, axis=2) - 1
        target = (slot + (jnp.arange(blocks, dtype=jnp.int32) * CAP)[:, None]).reshape(-1).astype(jnp.int32)
        expert_flat = flattened.reshape(-1).astype(jnp.int32)
        slot_owner = jnp.full((expert_count, blocks * CAP), tokens, jnp.int32).at[expert_flat, target].set(owner_ids)
        rows_pad = jnp.concatenate([layer_in, jnp.zeros((1, width), jnp.bfloat16)], axis=0)
        adj_pad = jnp.concatenate([adjoint.astype(jnp.bfloat16), jnp.zeros((1, width), jnp.bfloat16)], axis=0)

        def per_expert(packed):
            row_index, weight_in, weight_out = packed
            state_rows = rows_pad[row_index]
            adjoint_rows = adj_pad[row_index]
            preact = jnp.dot(state_rows, weight_in, preferred_element_type=jnp.float32)
            back = lax.dot_general(adjoint_rows, weight_out, (((1,), (1,)), ((), ())), preferred_element_type=jnp.float32)
            hidden = (back * gelu_slope(preact)).astype(jnp.bfloat16)
            return lax.dot_general(hidden, weight_in, (((1,), (1,)), ((), ())), preferred_element_type=jnp.float32).astype(jnp.bfloat16)

        results = lax.map(per_expert, (slot_owner, w_in, w_out))
        picked = results[expert_flat, target].reshape(tokens, TOP, width).astype(jnp.float32)
        combined = jnp.sum(step_gates[:, :, None] * picked, axis=1)
        updated = adjoint + step_size * combined
        return updated, updated

    _, outputs = lax.scan(one_step, terminal, (states, gates, routes), reverse=True)
    return outputs
```

```python
import functools

import jax
import jax.numpy as jnp
from jax import lax
from jax.experimental import pallas as pl
from jax.experimental.pallas import tpu as pltpu
from jax.sharding import PartitionSpec as P

MB = 32
CHUNKS = 4
LAG = 1
STEP_SIZE = 0.5
SLAB = 16
QUARTERS = 4


def gelu_slope(v):
    inside = 0.7978845608 * (v + 0.044715 * (v * v * v))
    t = jnp.tanh(inside)
    return 0.5 * (1.0 + t) + 0.5 * v * (1.0 - t * t) * 0.7978845608 * (
        1.0 + 3.0 * 0.044715 * v * v
    )


def kernel(
    steps, experts, fill, rows,
    states, terminal, rg, w_in, w_out,
    out,
    win, wout, adj, abf, araw, sts, psts, rgb, rgp, places, coefs, gather, scatter,
    send_a, recv_a, send_b, recv_b, recv_f, fsend, fsum, send_s, recv_s,
    slopes, back, hidden, rows_in, collect,
    w_sem, t_sem, loc_sem, l_sem, rg_ssem, rg_rsem, st_ssem, st_rsem, tb_ssem, tb_rsem,
    ar_ssem, ar_rsem, a_ssem, a_rsem, b_ssem, b_rsem, f_ssem, f_rsem, u_ssem, u_rsem,
    sr_ssem, sr_rsem, s_ssem, s_rsem, o_ssem, o_rsem,
):
    t = lax.axis_index("tm")
    me = lax.axis_index("expert")
    width = win.shape[0]
    ff = win.shape[1]
    dc = width // CHUNKS
    fc = ff // CHUNKS
    group = experts // 2
    hubs = group // 2
    flat = group * SLAB
    slots = experts * SLAB
    tails = range(fill, QUARTERS)
    bf = jnp.bfloat16
    f32 = jnp.float32

    side = me // group
    base = side * group
    spot = me - base
    lead = lax.rem(me, hubs)
    far_base = (1 - side) * group
    is_hub = (spot // hubs) != side
    my_half = spot // hubs
    far_hub = far_base + side * hubs + lead

    def near_spot(k):
        return lax.rem(spot + k, group)

    def near(k):
        return base + near_spot(k)

    def far_owner(v):
        return far_base + lead + v * hubs

    def hub_lead(k):
        return lax.rem(lead + k, hubs)

    def near_hub(k):
        return base + (1 - side) * hubs + hub_lead(k)

    def cols(c):
        return pl.ds(c * dc, dc)

    def tm_peer(k):
        return lax.rem(t + k, steps)

    def remote(src, dst, ssem, rsem, axis, dev):
        return pltpu.make_async_remote_copy(
            src_ref=src, dst_ref=dst, send_sem=ssem, recv_sem=rsem,
            device_id={axis: dev}, device_id_type=pl.DeviceIdType.MESH,
        )

    def block_rows(b):
        return pl.ds(pl.multiple_of(b * rows, rows), rows)

    own_terminal = []
    for c in range(CHUNKS):
        copy = pltpu.make_async_copy(terminal.at[block_rows(t), cols(c)], adj.at[c], t_sem.at[c])
        copy.start()
        own_terminal.append(copy)
    own_states = pltpu.make_async_copy(states.at[0, block_rows(t)], sts.at[t], loc_sem.at[0])
    own_states.start()
    own_rg = pltpu.make_async_copy(rg, rgb.at[t], loc_sem.at[1])
    own_rg.start()
    weights = []
    for c in range(CHUNKS):
        part = pl.ds(c * fc, fc)
        weights.append(pltpu.make_async_copy(w_in.at[0, :, part], win.at[:, part], w_sem.at[0, c]))
    for c in range(CHUNKS):
        weights.append(
            pltpu.make_async_copy(w_out.at[0, :, cols(c)], wout.at[:, cols(c)], w_sem.at[1, c])
        )
    for copy in weights:
        copy.start()

    barrier = pltpu.get_barrier_semaphore()
    for k in range(1, experts):
        pl.semaphore_signal(
            barrier, inc=1, device_id={"expert": lax.rem(me + k, experts)},
            device_id_type=pl.DeviceIdType.MESH,
        )
    for k in range(1, steps):
        pl.semaphore_signal(
            barrier, inc=1, device_id={"tm": tm_peer(k)}, device_id_type=pl.DeviceIdType.MESH
        )
    pl.semaphore_wait(barrier, experts + steps - 2)

    def rg_copy(k):
        return remote(rg, rgb.at[t], rg_ssem.at[k - 1], rg_rsem.at[t], "tm", tm_peer(k))

    def st_copy(k):
        b = tm_peer(k)
        return remote(
            states.at[0, block_rows(b)], sts.at[t], st_ssem.at[k - 1], st_rsem.at[t], "tm", b
        )

    def wait_rg(s):
        @pl.when(s == t)
        def _():
            own_rg.wait()

        @pl.when(s != t)
        def _():
            remote(rg, rgb.at[s], rg_ssem.at[0], rg_rsem.at[s], "tm", s).wait_recv()

    def wait_states(s):
        @pl.when(s == t)
        def _():
            own_states.wait()

        @pl.when(s != t)
        def _():
            remote(
                states.at[0, block_rows(s)], sts.at[s], st_ssem.at[0], st_rsem.at[s], "tm", s
            ).wait_recv()

    for k in range(1, steps):
        rg_copy(k).start()

    @pl.when(t == steps - 1)
    def _():
        for k in range(1, steps):
            st_copy(k).start()

    lane = lax.broadcasted_iota(jnp.int32, (rows, flat), 1)
    lane_expert = (lane // SLAB + base).astype(f32)
    place = lane % SLAB
    main_slot = jnp.where(place < 4 * fill, place, -1).astype(f32)

    def tail_slot(j, u):
        return jnp.where(place // 4 == u, 4 * j + place % 4, -1).astype(f32)

    earlier = (
        lax.broadcasted_iota(jnp.int32, (rows, rows), 1)
        < lax.broadcasted_iota(jnp.int32, (rows, rows), 0)
    ).astype(f32).astype(bf)
    tokens = rgb.shape[2]
    pick = lax.broadcasted_iota(jnp.int32, (rows, tokens), 1) == (
        t * rows + lax.broadcasted_iota(jnp.int32, (rows, tokens), 0)
    )

    def tables(source, s, blk):
        def column(n):
            return jnp.sum(jnp.where(pick, source[s, n : n + 1, :], 0.0), axis=1, keepdims=True)

        first = jnp.where(column(0) == lane_expert, 1.0, 0.0)
        second = jnp.where(column(1) == lane_expert, 1.0, 0.0)
        routed = first + second
        before = jnp.dot(earlier, routed.astype(bf), preferred_element_type=f32)
        weight = STEP_SIZE * (column(2) * first + column(3) * second)

        def pieces(slot):
            here = jnp.where(before == slot, 1.0, 0.0)
            scaled = weight * here
            high = scaled.astype(bf)
            low = (scaled - high.astype(f32)).astype(bf)
            return routed * here, [high, low]

        main, main_coefs = pieces(main_slot)
        for j in range(fill):
            chosen = [main]
            scales = list(main_coefs)
            for u in tails:
                tail, tail_coefs = pieces(tail_slot(j, u))
                chosen.append(tail)
                scales.extend(tail_coefs)
            places[s, blk, j] = jnp.concatenate(chosen, axis=0).T.astype(bf)
            coefs[s, blk, j] = jnp.concatenate(scales, axis=0)

    def pack(s, blk, source, wide, target):
        qw = wide // QUARTERS
        for j in range(fill):
            stack = jnp.concatenate(
                [source(j * qw, qw)] + [source(u * qw, qw) for u in tails], axis=0
            )
            block = jnp.dot(places[s, blk, j], stack, preferred_element_type=f32)
            target[:, :, j * qw : (j + 1) * qw] = block.astype(bf).reshape(group, SLAB, qw)

    def unpack(piece):
        qw = piece.shape[2] // fill
        flatter = piece.reshape(slots, fill * qw)
        stack = jnp.concatenate([flatter[:, j * qw : (j + 1) * qw] for j in range(fill)], axis=0)
        ends = [
            jnp.dot(gather[u - fill], stack, preferred_element_type=f32).astype(bf) for u in tails
        ]
        return jnp.concatenate([flatter] + ends, axis=1)

    def repack(answers, target):
        qw = answers.shape[1] // QUARTERS
        moved = None
        for u in tails:
            low = answers[:, u * qw : (u + 1) * qw].astype(bf)
            term = jnp.dot(scatter[u - fill], low, preferred_element_type=f32)
            moved = term if moved is None else moved + term
        upper = lax.broadcasted_iota(jnp.int32, (slots, qw), 0) % SLAB < 4 * fill
        for j in range(fill):
            block = jnp.where(
                upper, answers[:, j * qw : (j + 1) * qw], moved[j * slots : (j + 1) * slots]
            )
            target[:, :, j * qw : (j + 1) * qw] = block.astype(bf).reshape(experts, SLAB, qw)

    def combine(s, blk, piece):
        qw = piece.shape[2] // fill
        flatter = piece.reshape(flat, fill * qw)
        mains = []
        ends = [None for _ in tails]
        for j in range(fill):
            got = jnp.dot(
                coefs[s, blk, j], flatter[:, j * qw : (j + 1) * qw], preferred_element_type=f32
            )
            mains.append(got[:rows] + got[rows : 2 * rows])
            for n in range(len(ends)):
                at = 2 * rows * (n + 1)
                term = got[at : at + rows] + got[at + rows : at + 2 * rows]
                ends[n] = term if ends[n] is None else ends[n] + term
        return jnp.concatenate(mains + ends, axis=1)

    def a_raw(c):
        return remote(
            abf.at[c], araw.at[my_half, c], ar_ssem.at[c], ar_rsem.at[my_half, c], "expert", far_hub
        )

    def a_raw_in(c, v):
        return remote(
            abf.at[c], araw.at[v, c], ar_ssem.at[c], ar_rsem.at[v, c], "expert", far_hub
        )

    def a_own(c, k):
        return remote(
            send_a.at[c, 0, near_spot(k)], recv_a.at[c, spot],
            a_ssem.at[c, 0, k - 1], a_rsem.at[c, spot], "expert", near(k),
        )

    def far_slab(k, v):
        return group + 2 * hub_lead(k) + v

    def a_far(c, v, k):
        return remote(
            send_a.at[c, 1 + v, near_spot(k)], recv_a.at[c, far_slab(0, v)],
            a_ssem.at[c, 1 + v, k - 1], a_rsem.at[c, far_slab(0, v)], "expert", near(k),
        )

    def a_in(c, slab):
        return remote(
            send_a.at[c, 0, 0], recv_a.at[c, slab], a_ssem.at[c, 0, 0], a_rsem.at[c, slab],
            "expert", near(1),
        )

    def b_near(c, k):
        return remote(
            send_b.at[c, near_spot(k)], recv_b.at[c, spot],
            b_ssem.at[c, k - 1], b_rsem.at[c, spot], "expert", near(k),
        )

    def b_near_in(c, k):
        return remote(
            send_b.at[c, 0], recv_b.at[c, near_spot(k)],
            b_ssem.at[c, 0], b_rsem.at[c, near_spot(k)], "expert", near(k),
        )

    def b_far(c, k):
        return remote(
            send_b.at[c, pl.ds(far_slab(k, 0), 2)], recv_f.at[c, spot],
            f_ssem.at[c, k], f_rsem.at[c, spot], "expert", near_hub(k),
        )

    def b_far_in(c, k):
        return remote(
            send_b.at[c, pl.ds(group, 2)], recv_f.at[c, near_spot(k)],
            f_ssem.at[c, 0], f_rsem.at[c, near_spot(k)], "expert", near(k),
        )

    def u_copy(c, v):
        return remote(
            fsend.at[v, c], fsum.at[c], u_ssem.at[v, c], u_rsem.at[c], "expert", far_owner(v)
        )

    def s_raw(s):
        return remote(
            sts.at[s], psts.at[s, my_half], sr_ssem.at[s], sr_rsem.at[s, my_half], "expert", far_hub
        )

    def s_raw_in(s, v):
        return remote(
            sts.at[s], psts.at[s, v], sr_ssem.at[s], sr_rsem.at[s, v], "expert", far_hub
        )

    def s_own(s, k):
        return remote(
            send_s.at[s, 0, near_spot(k)], recv_s.at[s, spot],
            s_ssem.at[s, 0, k - 1], s_rsem.at[s, spot], "expert", near(k),
        )

    def s_far(s, v, k):
        return remote(
            send_s.at[s, 1 + v, near_spot(k)], recv_s.at[s, far_slab(0, v)],
            s_ssem.at[s, 1 + v, k - 1], s_rsem.at[s, far_slab(0, v)], "expert", near(k),
        )

    def s_in(s, slab):
        return remote(
            send_s.at[s, 0, 0], recv_s.at[s, slab], s_ssem.at[s, 0, 0], s_rsem.at[s, slab],
            "expert", near(1),
        )

    def tb_copy():
        return remote(rgb, rgp.at[my_half], tb_ssem.at[0], tb_rsem.at[my_half], "expert", far_hub)

    def tb_in(v):
        return remote(rgb, rgp.at[v], tb_ssem.at[0], tb_rsem.at[v], "expert", far_hub)

    def send_raw_a(c):
        abf[c] = adj[c].astype(bf)
        a_raw(c).start()

    def pack_own_a(s, c):
        pack(s, 0, lambda at, n: abf[c, :, at : at + n], dc, send_a.at[c, 0])
        for k in range(1, group):
            a_own(c, k).start()
        recv_a[c, spot] = send_a[c, 0, spot]

    def pack_far_a(s, c):
        for v in range(2):
            a_raw_in(c, v).wait_recv()
            pack(s, 1 + v, lambda at, n: araw[v, c, :, at : at + n], dc, send_a.at[c, 1 + v])
            for k in range(1, group):
                a_far(c, v, k).start()
            recv_a[c, far_slab(0, v)] = send_a[c, 1 + v, spot]

    def pack_own_s(s):
        pack(s, 0, lambda at, n: sts[s, :, at : at + n], width, send_s.at[s, 0])
        for k in range(1, group):
            s_own(s, k).start()
        recv_s[s, spot] = send_s[s, 0, spot]

    def pack_far_s(s):
        for v in range(2):
            s_raw_in(s, v).wait_recv()
            pack(s, 1 + v, lambda at, n: psts[s, v, :, at : at + n], width, send_s.at[s, 1 + v])
            for k in range(1, group):
                s_far(s, v, k).start()
            recv_s[s, far_slab(0, v)] = send_s[s, 1 + v, spot]

    def wait_slabs(copy_in):
        for k in range(1, group):
            copy_in(near_spot(k)).wait_recv()
        for k in range(1, hubs):
            for v in range(2):
                copy_in(far_slab(k, v)).wait_recv()

        @pl.when(jnp.logical_not(is_hub))
        def _():
            for v in range(2):
                copy_in(far_slab(0, v)).wait_recv()

    last = steps - 1
    for c in range(CHUNKS):
        own_terminal[c].wait()
        send_raw_a(c)

    row = lax.broadcasted_iota(jnp.int32, (slots, slots), 0)
    col = lax.broadcasted_iota(jnp.int32, (slots, slots), 1)
    for u in tails:
        for j in range(fill):
            shift = 4 * (u - j)
            take = jnp.logical_and(col == row + shift, (row % SLAB) // 4 == j)
            give = jnp.logical_and(row == col + shift, (col % SLAB) // 4 == j)
            span = slice(j * slots, (j + 1) * slots)
            gather[u - fill, :, span] = jnp.where(take, 1.0, 0.0).astype(bf)
            scatter[u - fill, span, :] = jnp.where(give, 1.0, 0.0).astype(bf)

    wait_rg(last)
    tables(rgb, last, 0)
    for c in range(CHUNKS):
        pack_own_a(last, c)
    for s in range(last):
        wait_rg(s)
    tb_copy().start()
    wait_states(last)
    s_raw(last).start()

    @pl.when(t != last)
    def _():
        for k in range(1, steps):
            st_copy(k).start()

    pack_own_s(last)
    tb_copy().wait_send()

    @pl.when(is_hub)
    def _():
        for v in range(2):
            tb_in(v).wait_recv()
            tables(rgp.at[v], last, 1 + v)
        for c in range(CHUNKS):
            pack_far_a(last, c)
        pack_far_s(last)

    for copy in weights:
        copy.wait()

    nt = (((1,), (1,)), ((), ()))

    def make_slopes(s):
        wait_slabs(lambda slab: s_in(s, slab))
        rows_in[...] = unpack(recv_s[s])
        for c in range(CHUNKS):
            part = pl.ds(c * fc, fc)
            pre = jnp.dot(rows_in[...], win[:, part], preferred_element_type=f32)
            slopes[:, part] = gelu_slope(pre)

    def out_remote(s, b, c):
        return remote(
            collect.at[s, c], out.at[0, block_rows(b), cols(c)],
            o_ssem.at[s, c], o_rsem.at[b, c], "tm", s,
        )

    def out_local(s, c):
        return pltpu.make_async_copy(
            collect.at[s, c], out.at[0, block_rows(t), cols(c)], l_sem.at[c]
        )

    def one_round(turn, carry):
        s = last - turn
        more = turn < last

        @pl.when(more)
        def _():
            wait_states(s - 1)
            s_raw(s - 1).start()
            tables(rgb, s - 1, 0)

        @pl.when(jnp.logical_and(more, is_hub))
        def _():
            for v in range(2):
                tables(rgp.at[v], s - 1, 1 + v)

        @pl.when(turn > 0)
        def _():
            make_slopes(s)

        for c in range(CHUNKS):
            wait_slabs(lambda slab: a_in(c, slab))
            term = lax.dot_general(
                unpack(recv_a[c]), wout[:, cols(c)], nt, preferred_element_type=f32
            )
            if c == 0:
                back[...] = term
            else:
                back[...] += term

        @pl.when(turn == 0)
        def _():
            make_slopes(s)

        hidden[...] = (back[...] * slopes[...]).astype(bf)
        for c in range(CHUNKS):
            answers = lax.dot_general(
                hidden[...], win[cols(c), :], nt, preferred_element_type=f32
            )
            repack(answers, send_b.at[c])
            for k in range(1, hubs):
                b_far(c, k).start()

            @pl.when(is_hub)
            def _():
                recv_f[c, spot] = send_b[c, pl.ds(far_slab(0, 0), 2)]

            @pl.when(jnp.logical_not(is_hub))
            def _():
                b_far(c, 0).start()

            for k in range(1, group):
                b_near(c, k).start()
            recv_b[c, spot] = send_b[c, spot]

        for c in range(CHUNKS):
            a_raw(c).wait_send()
            for k in range(1, group):
                a_own(c, k).wait_send()

        @pl.when(is_hub)
        def _():
            for c in range(CHUNKS):
                for v in range(2):
                    for k in range(1, group):
                        a_far(c, v, k).wait_send()

        @pl.when(more)
        def _():
            pack_own_s(s - 1)

        @pl.when(jnp.logical_and(more, is_hub))
        def _():
            pack_far_s(s - 1)

        def hub_sum(c):
            @pl.when(is_hub)
            def _():
                for k in range(1, group):
                    b_far_in(c, k).wait_recv()
                for v in range(2):
                    @pl.when(turn > 0)
                    def _():
                        u_copy(c, v).wait_send()

                    fsend[v, c] = combine(s, 1 + v, recv_f[c, :, v]).astype(bf)
                    u_copy(c, v).start()

        def finish(c):
            for k in range(1, group):
                b_near_in(c, k).wait_recv()
            mine = adj[c] + combine(s, 0, recv_b[c])
            remote(
                fsend.at[0, c], fsum.at[c], u_ssem.at[0, c], u_rsem.at[c], "expert", far_hub
            ).wait_recv()
            adj[c] = mine + fsum[c].astype(f32)
            collect[s, c] = adj[c]

            @pl.when(more)
            def _():
                send_raw_a(c)
                pack_own_a(s - 1, c)

            @pl.when(s == t)
            def _():
                out_local(s, c).start()

            @pl.when(s != t)
            def _():
                out_remote(s, t, c).start()

        for c in range(CHUNKS + LAG):
            if c < CHUNKS:
                hub_sum(c)
            if c >= LAG:
                finish(c - LAG)

        @pl.when(jnp.logical_and(more, is_hub))
        def _():
            for c in range(CHUNKS):
                pack_far_a(s - 1, c)

        for c in range(CHUNKS):
            for k in range(1, group):
                b_near(c, k).wait_send()
            for k in range(1, hubs):
                b_far(c, k).wait_send()

        @pl.when(jnp.logical_not(is_hub))
        def _():
            for c in range(CHUNKS):
                b_far(c, 0).wait_send()

        return carry

    lax.fori_loop(0, steps, one_round, 0)

    @pl.when(is_hub)
    def _():
        for c in range(CHUNKS):
            for v in range(2):
                u_copy(c, v).wait_send()
        for s in range(steps):
            for v in range(2):
                for k in range(1, group):
                    s_far(s, v, k).wait_send()

    for s in range(steps):
        s_raw(s).wait_send()
        for k in range(1, group):
            s_own(s, k).wait_send()
    for c in range(CHUNKS):
        out_local(t, c).wait()
    for k in range(1, steps):
        rg_copy(k).wait_send()
        st_copy(k).wait_send()
        b = tm_peer(k)
        for c in range(CHUNKS):
            out_remote(b, t, c).wait_send()
            out_remote(b, b, c).wait_recv()


def per_device(states, terminal, gates, routes, w_in, w_out):
    steps = lax.axis_size("tm")
    experts = lax.axis_size("expert")
    width = states.shape[2]
    ff = w_in.shape[2]
    top = routes.shape[2]
    tokens = states.shape[1]
    rows = tokens // steps
    cap = min(rows, (3 * MB * top + 2 * experts - 1) // (2 * experts))
    fill = -(-cap // 4)
    assert top == 2 and fill < QUARTERS and experts % 4 == 0
    group = experts // 2
    hubs = group // 2
    flat = group * SLAB
    slots = experts * SLAB
    dc = width // CHUNKS
    pc = dc * fill // QUARTERS
    ps = width * fill // QUARTERS
    kinds = 1 + QUARTERS - fill
    rg = jnp.concatenate([routes[0].T.astype(jnp.float32), gates[0].T], axis=0)
    dma = pltpu.SemaphoreType.DMA
    bf = jnp.bfloat16
    f32 = jnp.float32
    vm = pltpu.VMEM
    return pl.pallas_call(
        functools.partial(kernel, steps, experts, fill, rows),
        out_shape=jax.ShapeDtypeStruct(states.shape, f32),
        in_specs=[pl.BlockSpec(memory_space=pl.ANY)] * 5,
        out_specs=pl.BlockSpec(memory_space=pl.ANY),
        scratch_shapes=[
            vm((width, ff), bf),
            vm((ff, width), bf),
            vm((CHUNKS, rows, dc), f32),
            vm((CHUNKS, rows, dc), bf),
            vm((2, CHUNKS, rows, dc), bf),
            vm((steps, rows, width), bf),
            vm((steps, 2, rows, width), bf),
            vm((steps, 2 * top, tokens), f32),
            vm((2, steps, 2 * top, tokens), f32),
            vm((steps, 3, fill, flat, kinds * rows), bf),
            vm((steps, 3, fill, 2 * kinds * rows, flat), bf),
            vm((QUARTERS - fill, slots, fill * slots), bf),
            vm((QUARTERS - fill, fill * slots, slots), bf),
            vm((CHUNKS, 3, group, SLAB, pc), bf),
            vm((CHUNKS, experts, SLAB, pc), bf),
            vm((CHUNKS, experts, SLAB, pc), bf),
            vm((CHUNKS, group, SLAB, pc), bf),
            vm((CHUNKS, group, 2, SLAB, pc), bf),
            vm((2, CHUNKS, rows, dc), bf),
            vm((CHUNKS, rows, dc), bf),
            vm((steps, 3, group, SLAB, ps), bf),
            vm((steps, experts, SLAB, ps), bf),
            vm((slots, ff), f32),
            vm((slots, ff), f32),
            vm((slots, ff), bf),
            vm((slots, width), bf),
            vm((steps, CHUNKS, rows, dc), f32),
            dma((2, CHUNKS)),
            dma((CHUNKS,)),
            dma((2,)),
            dma((CHUNKS,)),
            dma((steps - 1,)),
            dma((steps,)),
            dma((steps - 1,)),
            dma((steps,)),
            dma((1,)),
            dma((2,)),
            dma((CHUNKS,)),
            dma((2, CHUNKS)),
            dma((CHUNKS, 3, group - 1)),
            dma((CHUNKS, experts)),
            dma((CHUNKS, group - 1)),
            dma((CHUNKS, group)),
            dma((CHUNKS, hubs)),
            dma((CHUNKS, group)),
            dma((2, CHUNKS)),
            dma((CHUNKS,)),
            dma((steps,)),
            dma((steps, 2)),
            dma((steps, 3, group - 1)),
            dma((steps, experts)),
            dma((steps, CHUNKS)),
            dma((steps, CHUNKS)),
        ],
        compiler_params=pltpu.CompilerParams(
            collective_id=0, has_side_effects=True, vmem_limit_bytes=60 * 1024 * 1024
        ),
    )(states, terminal, rg, w_in, w_out)


def solution(mesh):
    placed = (
        P("tm", "expert", None),
        P("expert", None),
        P("tm", "expert", None),
        P("tm", "expert", None),
        P("expert", None, None),
        P("expert", None, None),
    )
    return jax.shard_map(
        per_device, mesh=mesh, in_specs=placed, out_specs=P("tm", "expert", None), check_vma=False
    )
```

```python
import functools

import jax
import jax.numpy as jnp
from jax import lax
from jax.experimental import pallas as pl
from jax.experimental.pallas import tpu as pltpu
from jax.sharding import PartitionSpec as P

MB = 32
CHUNKS = 2
LAG = 1
TURN = 256
STEP_SIZE = 0.5
SLAB = 16
QUARTERS = 4


def gelu_slope(v):
    inside = 0.7978845608 * (v + 0.044715 * (v * v * v))
    t = jnp.tanh(inside)
    return 0.5 * (1.0 + t) + 0.5 * v * (1.0 - t * t) * 0.7978845608 * (
        1.0 + 3.0 * 0.044715 * v * v
    )


def kernel(
    steps, experts, fill, rows,
    states, terminal, gates, routes, w_in, w_out,
    out,
    rg, rt, win, wout, win_t, wout_t, adj, abf, araw, sts, psts, rgb, rgp, places, coefs, gather, scatter,
    send_a, send_f, recv_a, send_b, recv_b, recv_f, fsend, fsum, send_s, send_q, recv_s,
    slopes, back, hidden, rows_in, collect,
    w_sem, t_sem, loc_sem, l_sem, rg_ssem, rg_rsem, st_ssem, st_rsem, tb_ssem, tb_rsem,
    sends, ar_rsem, a_rsem, b_rsem, f_rsem, u_rsem,
    sr_ssem, sr_rsem, s_ssem, q_ssem, s_rsem, o_ssem, o_rsem,
):
    t = lax.axis_index("tm")
    me = lax.axis_index("expert")
    width = win.shape[0]
    ff = win.shape[1]
    dc = width // CHUNKS
    fc = ff // CHUNKS
    group = experts // 2
    hubs = group // 2
    flat = group * SLAB
    slots = experts * SLAB
    tails = range(fill, QUARTERS)
    bf = jnp.bfloat16
    f32 = jnp.float32

    side = me // group
    base = side * group
    spot = me - base
    lead = lax.rem(me, hubs)
    far_base = (1 - side) * group
    is_hub = (spot // hubs) != side
    my_half = spot // hubs
    far_hub = far_base + side * hubs + lead

    def near_spot(k):
        return lax.rem(spot + k, group)

    def near(k):
        return base + near_spot(k)

    def far_owner(v):
        return far_base + lead + v * hubs

    def hub_lead(k):
        return lax.rem(lead + k, hubs)

    def near_hub(k):
        return base + (1 - side) * hubs + hub_lead(k)

    def cols(c):
        return pl.ds(c * dc, dc)

    def tm_peer(k):
        return lax.rem(t + k, steps)

    def remote(src, dst, ssem, rsem, axis, dev):
        return pltpu.make_async_remote_copy(
            src_ref=src, dst_ref=dst, send_sem=ssem, recv_sem=rsem,
            device_id={axis: dev}, device_id_type=pl.DeviceIdType.MESH,
        )

    def block_rows(b):
        return pl.ds(pl.multiple_of(b * rows, rows), rows)

    own_terminal = []
    for c in range(CHUNKS):
        copy = pltpu.make_async_copy(terminal.at[block_rows(t), cols(c)], adj.at[c], t_sem.at[c])
        copy.start()
        own_terminal.append(copy)
    own_states = pltpu.make_async_copy(states.at[0, block_rows(t)], sts.at[t], loc_sem.at[0])
    own_states.start()
    own_routes = pltpu.make_async_copy(routes, rt, loc_sem.at[1])
    own_routes.start()
    own_gates = pltpu.make_async_copy(gates, rg.at[2:4], loc_sem.at[2])
    own_gates.start()
    weights = []
    for c in range(CHUNKS):
        part = pl.ds(c * fc, fc)
        weights.append(pltpu.make_async_copy(w_in.at[0, :, part], win.at[:, part], w_sem.at[0, c]))
    for c in range(CHUNKS):
        weights.append(
            pltpu.make_async_copy(w_out.at[0, :, cols(c)], wout.at[:, cols(c)], w_sem.at[1, c])
        )
    for copy in weights[CHUNKS:] + weights[:CHUNKS]:
        copy.start()

    barrier = pltpu.get_barrier_semaphore()
    for k in range(1, experts):
        pl.semaphore_signal(
            barrier, inc=1, device_id={"expert": lax.rem(me + k, experts)},
            device_id_type=pl.DeviceIdType.MESH,
        )
    for k in range(1, steps):
        pl.semaphore_signal(
            barrier, inc=1, device_id={"tm": tm_peer(k)}, device_id_type=pl.DeviceIdType.MESH
        )
    own_routes.wait()
    own_gates.wait()
    rg[0:2] = rt[...].astype(f32)
    rgb[t] = rg[...]
    pl.semaphore_wait(barrier, experts + steps - 2)

    def rg_copy(k):
        return remote(rg, rgb.at[t], rg_ssem.at[k - 1], rg_rsem.at[t], "tm", tm_peer(k))

    def st_copy(k):
        b = tm_peer(k)
        return remote(
            states.at[0, block_rows(b)], sts.at[t], st_ssem.at[k - 1], st_rsem.at[t], "tm", b
        )

    def wait_rg(s):
        @pl.when(s != t)
        def _():
            remote(rg, rgb.at[s], rg_ssem.at[0], rg_rsem.at[s], "tm", s).wait_recv()

    def wait_states(s):
        @pl.when(s == t)
        def _():
            own_states.wait()

        @pl.when(s != t)
        def _():
            remote(
                states.at[0, block_rows(s)], sts.at[s], st_ssem.at[0], st_rsem.at[s], "tm", s
            ).wait_recv()

    for k in range(1, steps):
        rg_copy(k).start()

    @pl.when(t == steps - 1)
    def _():
        for k in range(1, steps):
            st_copy(k).start()

    lane = lax.broadcasted_iota(jnp.int32, (rows, flat), 1)
    lane_expert = (lane // SLAB + base).astype(f32)
    place = lane % SLAB
    main_slot = jnp.where(place < 4 * fill, place, -1).astype(f32)

    def tail_slot(j, u):
        return jnp.where(place // 4 == u, 4 * j + place % 4, -1).astype(f32)

    earlier = (
        lax.broadcasted_iota(jnp.int32, (rows, rows), 1)
        < lax.broadcasted_iota(jnp.int32, (rows, rows), 0)
    ).astype(f32).astype(bf)
    tokens = rgb.shape[2]
    pick = lax.broadcasted_iota(jnp.int32, (rows, tokens), 1) == (
        t * rows + lax.broadcasted_iota(jnp.int32, (rows, tokens), 0)
    )

    def tables(source, s, blk):
        def column(n):
            return jnp.sum(jnp.where(pick, source[s, n : n + 1, :], 0.0), axis=1, keepdims=True)

        first = jnp.where(column(0) == lane_expert, 1.0, 0.0)
        second = jnp.where(column(1) == lane_expert, 1.0, 0.0)
        routed = first + second
        before = jnp.dot(earlier, routed.astype(bf), preferred_element_type=f32)
        weight = STEP_SIZE * (column(2) * first + column(3) * second)

        def pieces(slot):
            here = jnp.where(before == slot, 1.0, 0.0)
            scaled = weight * here
            high = scaled.astype(bf)
            low = (scaled - high.astype(f32)).astype(bf)
            return routed * here, [high, low]

        main, main_coefs = pieces(main_slot)
        for j in range(fill):
            chosen = [main]
            scales = list(main_coefs)
            for u in tails:
                tail, tail_coefs = pieces(tail_slot(j, u))
                chosen.append(tail)
                scales.extend(tail_coefs)
            places[s, blk, j] = jnp.concatenate(chosen, axis=0).T.astype(bf)
            coefs[s, blk, j] = jnp.concatenate(scales, axis=0)

    def pack(s, blk, source, wide, target):
        qw = wide // QUARTERS
        for j in range(fill):
            stack = jnp.concatenate(
                [source(j * qw, qw)] + [source(u * qw, qw) for u in tails], axis=0
            )
            block = jnp.dot(places[s, blk, j], stack, preferred_element_type=f32)
            target[:, :, j * qw : (j + 1) * qw] = block.astype(bf).reshape(group, SLAB, qw)

    def unpack(piece):
        qw = piece.shape[2] // fill
        flatter = piece.reshape(slots, fill * qw)
        stack = jnp.concatenate([flatter[:, j * qw : (j + 1) * qw] for j in range(fill)], axis=0)
        ends = [
            jnp.dot(gather[u - fill], stack, preferred_element_type=f32).astype(bf) for u in tails
        ]
        return jnp.concatenate([flatter] + ends, axis=1)

    def repack(answers, target):
        qw = answers.shape[1] // QUARTERS
        moved = None
        for u in tails:
            low = answers[:, u * qw : (u + 1) * qw].astype(bf)
            term = jnp.dot(scatter[u - fill], low, preferred_element_type=f32)
            moved = term if moved is None else moved + term
        upper = lax.broadcasted_iota(jnp.int32, (slots, qw), 0) % SLAB < 4 * fill
        for j in range(fill):
            block = jnp.where(
                upper, answers[:, j * qw : (j + 1) * qw], moved[j * slots : (j + 1) * slots]
            )
            target[:, :, j * qw : (j + 1) * qw] = block.astype(bf).reshape(experts, SLAB, qw)

    def combine(s, blk, piece):
        qw = piece.shape[2] // fill
        flatter = piece.reshape(flat, fill * qw)
        mains = []
        ends = [None for _ in tails]
        for j in range(fill):
            got = jnp.dot(
                coefs[s, blk, j], flatter[:, j * qw : (j + 1) * qw], preferred_element_type=f32
            )
            mains.append(got[:rows] + got[rows : 2 * rows])
            for n in range(len(ends)):
                at = 2 * rows * (n + 1)
                term = got[at : at + rows] + got[at + rows : at + 2 * rows]
                ends[n] = term if ends[n] is None else ends[n] + term
        return jnp.concatenate(mains + ends, axis=1)

    def far_slab(k):
        return group + 2 * hub_lead(k)

    def a_raw(c, v=None):
        v = my_half if v is None else v
        return remote(abf.at[c], araw.at[v, c], sends.at[0], ar_rsem.at[v, c], "expert", far_hub)

    def a_own(c, k):
        return remote(
            send_a.at[c, near_spot(k)], recv_a.at[c, spot],
            sends.at[1], a_rsem.at[c], "expert", near(k),
        )

    def a_far(c, k):
        return remote(
            send_f.at[c, near_spot(k)], recv_a.at[c, pl.ds(far_slab(0), 2)],
            sends.at[2], a_rsem.at[c], "expert", near(k),
        )

    def a_in(c, count):
        return remote(
            send_b.at[c, 0:count], recv_a.at[c, 0:count], sends.at[1], a_rsem.at[c],
            "expert", near(1),
        )

    def b_near(c, k):
        return remote(
            send_b.at[c, near_spot(k)], recv_b.at[c, spot],
            sends.at[3], b_rsem.at[c], "expert", near(k),
        )

    def b_near_in(c):
        return remote(
            send_b.at[c, 1:group], recv_b.at[c, 1:group],
            sends.at[3], b_rsem.at[c], "expert", near(1),
        )

    def b_far(c, k):
        return remote(
            send_b.at[c, pl.ds(far_slab(k), 2)], recv_f.at[c, spot],
            sends.at[4], f_rsem.at[c], "expert", near_hub(k),
        )

    def b_far_in(c):
        return remote(
            send_f.at[c, 1:group], recv_f.at[c, 1:group],
            sends.at[4], f_rsem.at[c], "expert", near(1),
        )

    def u_copy(c, v):
        return remote(
            fsend.at[c, v], fsum.at[c], sends.at[5], u_rsem.at[c], "expert", far_owner(v)
        )

    def sent(ref, sem, dev):
        remote(ref, ref, sem, sem, "expert", dev).wait_send()

    def s_raw(s, v=None):
        v = my_half if v is None else v
        return remote(
            sts.at[s], psts.at[s, v], sr_ssem.at[s], sr_rsem.at[s, v], "expert", far_hub
        )

    def s_own(s, k):
        return remote(
            send_s.at[s, near_spot(k)], recv_s.at[s, spot],
            s_ssem.at[s], s_rsem.at[s], "expert", near(k),
        )

    def s_far(s, k):
        return remote(
            send_q.at[s, near_spot(k)], recv_s.at[s, pl.ds(far_slab(0), 2)],
            q_ssem.at[s], s_rsem.at[s], "expert", near(k),
        )

    def s_in(s, count):
        return remote(
            recv_s.at[s, 0:count], recv_s.at[s, 0:count], s_ssem.at[s], s_rsem.at[s],
            "expert", near(1),
        )

    def tb_copy():
        return remote(rgb, rgp.at[my_half], tb_ssem.at[0], tb_rsem.at[my_half], "expert", far_hub)

    def tb_in(v):
        return remote(rgb, rgp.at[v], tb_ssem.at[0], tb_rsem.at[v], "expert", far_hub)

    def send_raw_a(c):
        abf[c] = adj[c].astype(bf)
        a_raw(c).start()

    def pack_own_a(s, c):
        pack(s, 0, lambda at, n: abf[c, :, at : at + n], dc, send_a.at[c])
        for k in range(1, group):
            a_own(c, k).start()
        recv_a[c, spot] = send_a[c, spot]

    def pack_far_a(s, c):
        for v in range(2):
            a_raw(c, v).wait_recv()
            pack(s, 1 + v, lambda at, n: araw[v, c, :, at : at + n], dc, send_f.at[c, :, v])
        for k in range(1, group):
            a_far(c, k).start()
        recv_a[c, pl.ds(far_slab(0), 2)] = send_f[c, spot]

    def pack_own_s(s):
        pack(s, 0, lambda at, n: sts[s, :, at : at + n], width, send_s.at[s])
        for k in range(1, group):
            s_own(s, k).start()
        recv_s[s, spot] = send_s[s, spot]

    def pack_far_s(s):
        for v in range(2):
            s_raw(s, v).wait_recv()
            pack(s, 1 + v, lambda at, n: psts[s, v, :, at : at + n], width, send_q.at[s, :, v])
        for k in range(1, group):
            s_far(s, k).start()
        recv_s[s, pl.ds(far_slab(0), 2)] = send_q[s, spot]

    def wait_slabs(copy_in):
        @pl.when(is_hub)
        def _():
            copy_in(group - 1 + 2 * (hubs - 1)).wait_recv()

        @pl.when(jnp.logical_not(is_hub))
        def _():
            copy_in(group - 1 + 2 * hubs).wait_recv()

    last = steps - 1
    late = lax.rem(t, 2) == 1
    early = lax.rem(t, 2) == 0

    def turn_over(source, target):
        def body(n, carry):
            at = pl.multiple_of(n * TURN, TURN)
            for m in range(0, source.shape[1], TURN):
                target[m : m + TURN, pl.ds(at, TURN)] = source[pl.ds(at, TURN), m : m + TURN].T
            return carry

        lax.fori_loop(0, source.shape[0] // TURN, body, 0)

    def turn_out():
        for copy in weights[CHUNKS:]:
            copy.wait()
        turn_over(wout, wout_t)

    def turn_in():
        for copy in weights[:CHUNKS]:
            copy.wait()
        turn_over(win, win_t)

    def send_all_raw_a():
        for c in range(CHUNKS):
            own_terminal[c].wait()
            send_raw_a(c)

    @pl.when(early)
    def _():
        send_all_raw_a()

    row = lax.broadcasted_iota(jnp.int32, (slots, slots), 0)
    col = lax.broadcasted_iota(jnp.int32, (slots, slots), 1)
    for u in tails:
        for j in range(fill):
            shift = 4 * (u - j)
            take = jnp.logical_and(col == row + shift, (row % SLAB) // 4 == j)
            give = jnp.logical_and(row == col + shift, (col % SLAB) // 4 == j)
            span = slice(j * slots, (j + 1) * slots)
            gather[u - fill, :, span] = jnp.where(take, 1.0, 0.0).astype(bf)
            scatter[u - fill, span, :] = jnp.where(give, 1.0, 0.0).astype(bf)

    wait_rg(last)
    tables(rgb, last, 0)

    @pl.when(early)
    def _():
        for c in range(CHUNKS):
            pack_own_a(last, c)

    for s in range(last):
        wait_rg(s)
    tb_copy().start()

    @pl.when(t != last)
    def _():
        for k in range(1, steps):
            st_copy(k).start()

    @pl.when(late)
    def _():
        turn_out()
        turn_in()
        send_all_raw_a()
        for c in range(CHUNKS):
            pack_own_a(last, c)

    wait_states(last)
    s_raw(last).start()
    pack_own_s(last)
    tb_copy().wait_send()

    @pl.when(is_hub)
    def _():
        for v in range(2):
            tb_in(v).wait_recv()
            tables(rgp.at[v], last, 1 + v)
        for c in range(CHUNKS):
            pack_far_a(last, c)
        pack_far_s(last)

    @pl.when(early)
    def _():
        turn_out()
        turn_in()

    def slope_rows(s):
        wait_slabs(lambda count: s_in(s, count))
        rows_in[...] = unpack(recv_s[s])

    def slope_part(c):
        part = pl.ds(c * fc, fc)
        pre = jnp.dot(rows_in[...], win[:, part], preferred_element_type=f32)
        slopes[:, part] = gelu_slope(pre)

    def out_remote(s, b, c):
        return remote(
            collect.at[s, c], out.at[0, block_rows(b), cols(c)],
            o_ssem.at[s, c], o_rsem.at[b, c], "tm", s,
        )

    def out_local(s, c):
        return pltpu.make_async_copy(
            collect.at[s, c], out.at[0, block_rows(t), cols(c)], l_sem.at[c]
        )

    def one_round(turn, carry):
        s = last - turn
        more = turn < last

        @pl.when(more)
        def _():
            wait_states(s - 1)
            s_raw(s - 1).start()
            tables(rgb, s - 1, 0)

        @pl.when(jnp.logical_and(more, is_hub))
        def _():
            for v in range(2):
                tables(rgp.at[v], s - 1, 1 + v)

        @pl.when(turn > 0)
        def _():
            slope_rows(s)
            for c in range(CHUNKS):
                slope_part(c)

        for c in range(CHUNKS):
            wait_slabs(lambda count: a_in(c, count))
            term = jnp.dot(unpack(recv_a[c]), wout_t[cols(c), :], preferred_element_type=f32)
            if c == 0:
                back[...] = term
            else:
                back[...] += term

        @pl.when(turn == 0)
        def _():
            slope_rows(s)
            for c in range(CHUNKS):
                slope_part(c)

        hidden[...] = (back[...] * slopes[...]).astype(bf)
        for c in range(CHUNKS):
            answers = jnp.dot(hidden[...], win_t[:, cols(c)], preferred_element_type=f32)
            repack(answers, send_b.at[c])
            for k in range(1, hubs):
                b_far(c, k).start()

            @pl.when(is_hub)
            def _():
                recv_f[c, spot] = send_b[c, pl.ds(far_slab(0), 2)]

            @pl.when(jnp.logical_not(is_hub))
            def _():
                b_far(c, 0).start()

            for k in range(1, group):
                b_near(c, k).start()
            recv_b[c, spot] = send_b[c, spot]

        sent(abf, sends.at[0], far_hub)
        sent(send_a.at[:, 1:group], sends.at[1], near(1))

        @pl.when(is_hub)
        def _():
            sent(send_f.at[:, 1:group], sends.at[2], near(1))

        @pl.when(more)
        def _():
            pack_own_s(s - 1)

        @pl.when(jnp.logical_and(more, is_hub))
        def _():
            pack_far_s(s - 1)

        def hub_sum(c):
            @pl.when(is_hub)
            def _():
                b_far_in(c).wait_recv()
                for v in range(2):
                    fsend[c, v] = combine(s, 1 + v, recv_f[c, :, v]).astype(bf)
                    u_copy(c, v).start()

        def finish(c):
            b_near_in(c).wait_recv()
            mine = adj[c] + combine(s, 0, recv_b[c])
            u_copy(c, 0).wait_recv()
            adj[c] = mine + fsum[c].astype(f32)
            collect[s, c] = adj[c]

            @pl.when(more)
            def _():
                send_raw_a(c)
                pack_own_a(s - 1, c)

            @pl.when(s == t)
            def _():
                out_local(s, c).start()

            @pl.when(s != t)
            def _():
                out_remote(s, t, c).start()

        for c in range(CHUNKS + LAG):
            if c < CHUNKS:
                hub_sum(c)
            if c >= LAG:
                finish(c - LAG)

        @pl.when(jnp.logical_and(more, is_hub))
        def _():
            for c in range(CHUNKS):
                pack_far_a(s - 1, c)

        sent(send_b.at[:, 1:group], sends.at[3], near(1))

        @pl.when(is_hub)
        def _():
            if hubs > 1:
                sent(send_b.at[:, 0 : 2 * (hubs - 1)], sends.at[4], near(1))
            sent(fsend, sends.at[5], far_hub)

        @pl.when(jnp.logical_not(is_hub))
        def _():
            sent(send_b.at[:, 0 : 2 * hubs], sends.at[4], near(1))

        return carry

    lax.fori_loop(0, steps, one_round, 0)

    for s in range(steps):
        s_raw(s).wait_send()
        sent(send_s.at[s, 1:group], s_ssem.at[s], near(1))

        @pl.when(is_hub)
        def _():
            sent(send_q.at[s, 1:group], q_ssem.at[s], near(1))

    for c in range(CHUNKS):
        out_local(t, c).wait()
    for k in range(1, steps):
        rg_copy(k).wait_send()
        st_copy(k).wait_send()
        b = tm_peer(k)
        for c in range(CHUNKS):
            out_remote(b, t, c).wait_send()
            out_remote(b, b, c).wait_recv()


def per_device(states, terminal, gates, routes, w_in, w_out):
    steps = lax.axis_size("tm")
    experts = lax.axis_size("expert")
    width = states.shape[2]
    ff = w_in.shape[2]
    top = routes.shape[2]
    tokens = states.shape[1]
    rows = tokens // steps
    cap = min(rows, (3 * MB * top + 2 * experts - 1) // (2 * experts))
    fill = -(-cap // 4)
    assert top == 2 and fill < QUARTERS and experts % 4 == 0
    group = experts // 2
    hubs = group // 2
    flat = group * SLAB
    slots = experts * SLAB
    dc = width // CHUNKS
    pc = dc * fill // QUARTERS
    ps = width * fill // QUARTERS
    kinds = 1 + QUARTERS - fill
    dma = pltpu.SemaphoreType.DMA
    bf = jnp.bfloat16
    f32 = jnp.float32
    vm = pltpu.VMEM
    return pl.pallas_call(
        functools.partial(kernel, steps, experts, fill, rows),
        out_shape=jax.ShapeDtypeStruct(states.shape, f32),
        in_specs=[pl.BlockSpec(memory_space=pl.ANY)] * 6,
        out_specs=pl.BlockSpec(memory_space=pl.ANY),
        scratch_shapes=[
            vm((2 * top, tokens), f32),
            vm((top, tokens), jnp.int32),
            vm((width, ff), bf),
            vm((ff, width), bf),
            vm((ff, width), bf),
            vm((width, ff), bf),
            vm((CHUNKS, rows, dc), f32),
            vm((CHUNKS, rows, dc), bf),
            vm((2, CHUNKS, rows, dc), bf),
            vm((steps, rows, width), bf),
            vm((steps, 2, rows, width), bf),
            vm((steps, 2 * top, tokens), f32),
            vm((2, steps, 2 * top, tokens), f32),
            vm((steps, 3, fill, flat, kinds * rows), bf),
            vm((steps, 3, fill, 2 * kinds * rows, flat), bf),
            vm((QUARTERS - fill, slots, fill * slots), bf),
            vm((QUARTERS - fill, fill * slots, slots), bf),
            vm((CHUNKS, group, SLAB, pc), bf),
            vm((CHUNKS, group, 2, SLAB, pc), bf),
            vm((CHUNKS, experts, SLAB, pc), bf),
            vm((CHUNKS, experts, SLAB, pc), bf),
            vm((CHUNKS, group, SLAB, pc), bf),
            vm((CHUNKS, group, 2, SLAB, pc), bf),
            vm((CHUNKS, 2, rows, dc), bf),
            vm((CHUNKS, rows, dc), bf),
            vm((steps, group, SLAB, ps), bf),
            vm((steps, group, 2, SLAB, ps), bf),
            vm((steps, experts, SLAB, ps), bf),
            vm((slots, ff), f32),
            vm((slots, ff), f32),
            vm((slots, ff), bf),
            vm((slots, width), bf),
            vm((steps, CHUNKS, rows, dc), f32),
            dma((2, CHUNKS)),
            dma((CHUNKS,)),
            dma((3,)),
            dma((CHUNKS,)),
            dma((steps - 1,)),
            dma((steps,)),
            dma((steps - 1,)),
            dma((steps,)),
            dma((1,)),
            dma((2,)),
            dma((6,)),
            dma((2, CHUNKS)),
            dma((CHUNKS,)),
            dma((CHUNKS,)),
            dma((CHUNKS,)),
            dma((CHUNKS,)),
            dma((steps,)),
            dma((steps, 2)),
            dma((steps,)),
            dma((steps,)),
            dma((steps,)),
            dma((steps, CHUNKS)),
            dma((steps, CHUNKS)),
        ],
        compiler_params=pltpu.CompilerParams(
            collective_id=0, has_side_effects=True, vmem_limit_bytes=60 * 1024 * 1024
        ),
    )(states, terminal, gates[0].T, routes[0].T, w_in, w_out)


def solution(mesh):
    placed = (
        P("tm", "expert", None),
        P("expert", None),
        P("tm", "expert", None),
        P("tm", "expert", None),
        P("expert", None, None),
        P("expert", None, None),
    )
    return jax.shard_map(
        per_device, mesh=mesh, in_specs=placed, out_specs=P("tm", "expert", None), check_vma=False
    )
```

```python
import functools

import jax
import jax.numpy as jnp
from jax import lax
from jax.experimental import pallas as pl
from jax.experimental.pallas import tpu as pltpu
from jax.sharding import PartitionSpec as P

MB = 32
CHUNKS = 2
TURN = 256
STEP_SIZE = 0.5
SLAB = 16
QUARTERS = 4


def gelu_slope(v):
    inside = 0.7978845608 * (v + 0.044715 * (v * v * v))
    t = jnp.tanh(inside)
    return 0.5 * (1.0 + t) + 0.5 * v * (1.0 - t * t) * 0.7978845608 * (
        1.0 + 3.0 * 0.044715 * v * v
    )


def kernel(
    steps, experts, fill, rows,
    states, terminal, gates, routes, w_in, w_out,
    out,
    rg, rt, win, wout, win_t, wout_t, adj, abf, araw, sts, psts, rgb, rgp, places, coefs, gather, scatter,
    send_a, send_f, recv_a, send_b, recv_b, send_s, send_q, recv_s,
    slopes, back, hidden, rows_in, collect,
    w_sem, t_sem, loc_sem, l_sem, rg_ssem, rg_rsem, st_ssem, st_rsem, tb_ssem, tb_rsem,
    sends, ar_rsem, a_rsem, b_rsem,
    sr_ssem, sr_rsem, s_ssem, q_ssem, s_rsem, o_ssem, o_rsem,
):
    t = lax.axis_index("tm")
    me = lax.axis_index("expert")
    width = win.shape[0]
    ff = win.shape[1]
    dc = width // CHUNKS
    fc = ff // CHUNKS
    group = experts // 2
    hubs = group // 2
    flat = group * SLAB
    slots = experts * SLAB
    tails = range(fill, QUARTERS)
    bf = jnp.bfloat16
    f32 = jnp.float32

    side = me // group
    base = side * group
    spot = me - base
    lead = lax.rem(me, hubs)
    far_base = (1 - side) * group
    is_hub = (spot // hubs) != side
    my_half = spot // hubs
    far_hub = far_base + side * hubs + lead

    def near_spot(k):
        return lax.rem(spot + k, group)

    def near(k):
        return base + near_spot(k)

    def far_owner(v):
        return far_base + lead + v * hubs

    def hub_lead(k):
        return lax.rem(lead + k, hubs)

    def near_hub(k):
        return base + (1 - side) * hubs + hub_lead(k)

    def cols(c):
        return pl.ds(c * dc, dc)

    def tm_peer(k):
        return lax.rem(t + k, steps)

    def remote(src, dst, ssem, rsem, axis, dev):
        return pltpu.make_async_remote_copy(
            src_ref=src, dst_ref=dst, send_sem=ssem, recv_sem=rsem,
            device_id={axis: dev}, device_id_type=pl.DeviceIdType.MESH,
        )

    def block_rows(b):
        return pl.ds(pl.multiple_of(b * rows, rows), rows)

    own_terminal = []
    for c in range(CHUNKS):
        copy = pltpu.make_async_copy(terminal.at[block_rows(t), cols(c)], adj.at[c], t_sem.at[c])
        copy.start()
        own_terminal.append(copy)
    own_states = pltpu.make_async_copy(states.at[0, block_rows(t)], sts.at[t], loc_sem.at[0])
    own_states.start()
    own_routes = pltpu.make_async_copy(routes, rt, loc_sem.at[1])
    own_routes.start()
    own_gates = pltpu.make_async_copy(gates, rg.at[2:4], loc_sem.at[2])
    own_gates.start()
    weights = []
    for c in range(CHUNKS):
        part = pl.ds(c * fc, fc)
        weights.append(pltpu.make_async_copy(w_in.at[0, :, part], win.at[:, part], w_sem.at[0, c]))
    for c in range(CHUNKS):
        weights.append(
            pltpu.make_async_copy(w_out.at[0, :, cols(c)], wout.at[:, cols(c)], w_sem.at[1, c])
        )
    for copy in weights[CHUNKS:] + weights[:CHUNKS]:
        copy.start()

    barrier = pltpu.get_barrier_semaphore()
    for k in range(1, experts):
        pl.semaphore_signal(
            barrier, inc=1, device_id={"expert": lax.rem(me + k, experts)},
            device_id_type=pl.DeviceIdType.MESH,
        )
    for k in range(1, steps):
        pl.semaphore_signal(
            barrier, inc=1, device_id={"tm": tm_peer(k)}, device_id_type=pl.DeviceIdType.MESH
        )
    own_routes.wait()
    own_gates.wait()
    rg[0:2] = rt[...].astype(f32)
    rgb[t] = rg[...]
    pl.semaphore_wait(barrier, experts + steps - 2)

    def rg_copy(k):
        return remote(rg, rgb.at[t], rg_ssem.at[k - 1], rg_rsem.at[t], "tm", tm_peer(k))

    def st_copy(k):
        b = tm_peer(k)
        return remote(
            states.at[0, block_rows(b)], sts.at[t], st_ssem.at[k - 1], st_rsem.at[t], "tm", b
        )

    def wait_rg(s):
        @pl.when(s != t)
        def _():
            remote(rg, rgb.at[s], rg_ssem.at[0], rg_rsem.at[s], "tm", s).wait_recv()

    def wait_states(s):
        @pl.when(s == t)
        def _():
            own_states.wait()

        @pl.when(s != t)
        def _():
            remote(
                states.at[0, block_rows(s)], sts.at[s], st_ssem.at[0], st_rsem.at[s], "tm", s
            ).wait_recv()

    for k in range(1, steps):
        rg_copy(k).start()

    @pl.when(t == steps - 1)
    def _():
        for k in range(1, steps):
            st_copy(k).start()

    lane = lax.broadcasted_iota(jnp.int32, (rows, flat), 1)
    near_expert = (lane // SLAB + base).astype(f32)
    far_expert = (lane // SLAB + far_base).astype(f32)
    place = lane % SLAB
    main_slot = jnp.where(place < 4 * fill, place, -1).astype(f32)

    def tail_slot(j, u):
        return jnp.where(place // 4 == u, 4 * j + place % 4, -1).astype(f32)

    earlier = (
        lax.broadcasted_iota(jnp.int32, (rows, rows), 1)
        < lax.broadcasted_iota(jnp.int32, (rows, rows), 0)
    ).astype(f32).astype(bf)
    tokens = rgb.shape[2]
    pick = lax.broadcasted_iota(jnp.int32, (rows, tokens), 1) == (
        t * rows + lax.broadcasted_iota(jnp.int32, (rows, tokens), 0)
    )

    def tables(source, s, blk):
        lane_expert = far_expert if blk == 3 else near_expert

        def column(n):
            return jnp.sum(jnp.where(pick, source[s, n : n + 1, :], 0.0), axis=1, keepdims=True)

        first = jnp.where(column(0) == lane_expert, 1.0, 0.0)
        second = jnp.where(column(1) == lane_expert, 1.0, 0.0)
        routed = first + second
        before = jnp.dot(earlier, routed.astype(bf), preferred_element_type=f32)
        weight = STEP_SIZE * (column(2) * first + column(3) * second)

        def pieces(slot):
            here = jnp.where(before == slot, 1.0, 0.0)
            scaled = weight * here
            high = scaled.astype(bf)
            low = (scaled - high.astype(f32)).astype(bf)
            return routed * here, [high, low]

        main, main_coefs = pieces(main_slot)
        for j in range(fill):
            chosen = [main]
            scales = list(main_coefs)
            for u in tails:
                tail, tail_coefs = pieces(tail_slot(j, u))
                chosen.append(tail)
                scales.extend(tail_coefs)
            if blk < 3:
                places[s, blk, j] = jnp.concatenate(chosen, axis=0).T.astype(bf)
            if blk % 3 == 0:
                coefs[s, blk // 3, j] = jnp.concatenate(scales, axis=0)

    def pack(s, blk, source, wide, target):
        qw = wide // QUARTERS
        for j in range(fill):
            stack = jnp.concatenate(
                [source(j * qw, qw)] + [source(u * qw, qw) for u in tails], axis=0
            )
            block = jnp.dot(places[s, blk, j], stack, preferred_element_type=f32)
            target[:, :, j * qw : (j + 1) * qw] = block.astype(bf).reshape(group, SLAB, qw)

    def unpack(piece):
        qw = piece.shape[2] // fill
        flatter = piece.reshape(slots, fill * qw)
        stack = jnp.concatenate([flatter[:, j * qw : (j + 1) * qw] for j in range(fill)], axis=0)
        ends = [
            jnp.dot(gather[u - fill], stack, preferred_element_type=f32).astype(bf) for u in tails
        ]
        return jnp.concatenate([flatter] + ends, axis=1)

    def repack(answers, target):
        qw = answers.shape[1] // QUARTERS
        moved = None
        for u in tails:
            low = answers[:, u * qw : (u + 1) * qw].astype(bf)
            term = jnp.dot(scatter[u - fill], low, preferred_element_type=f32)
            moved = term if moved is None else moved + term
        upper = lax.broadcasted_iota(jnp.int32, (slots, qw), 0) % SLAB < 4 * fill
        for j in range(fill):
            block = jnp.where(
                upper, answers[:, j * qw : (j + 1) * qw], moved[j * slots : (j + 1) * slots]
            )
            target[:, :, j * qw : (j + 1) * qw] = block.astype(bf).reshape(experts, SLAB, qw)

    def combine(s, blk, piece):
        qw = piece.shape[2] // fill
        flatter = piece.reshape(flat, fill * qw)
        mains = []
        ends = [None for _ in tails]
        for j in range(fill):
            got = jnp.dot(
                coefs[s, blk, j], flatter[:, j * qw : (j + 1) * qw], preferred_element_type=f32
            )
            mains.append(got[:rows] + got[rows : 2 * rows])
            for n in range(len(ends)):
                at = 2 * rows * (n + 1)
                term = got[at : at + rows] + got[at + rows : at + 2 * rows]
                ends[n] = term if ends[n] is None else ends[n] + term
        return jnp.concatenate(mains + ends, axis=1)

    def far_slab(k):
        return group + 2 * hub_lead(k)

    def a_raw(c, v=None):
        v = my_half if v is None else v
        return remote(abf.at[c], araw.at[v, c], sends.at[0], ar_rsem.at[v, c], "expert", far_hub)

    def a_own(c, k):
        return remote(
            send_a.at[c, near_spot(k)], recv_a.at[c, spot],
            sends.at[1], a_rsem.at[c], "expert", near(k),
        )

    def a_far(c, k):
        return remote(
            send_f.at[c, near_spot(k)], recv_a.at[c, pl.ds(far_slab(0), 2)],
            sends.at[2], a_rsem.at[c], "expert", near(k),
        )

    def a_in(c, count):
        return remote(
            send_b.at[c, 0:count], recv_a.at[c, 0:count], sends.at[1], a_rsem.at[c],
            "expert", near(1),
        )

    def b_near(c, k):
        return remote(
            send_b.at[c, near_spot(k)], recv_b.at[c, spot],
            sends.at[3], b_rsem.at[c], "expert", near(k),
        )

    def b_in(c):
        return remote(
            send_b.at[c, 1:experts], recv_b.at[c, 1:experts],
            sends.at[3], b_rsem.at[c], "expert", near(1),
        )

    def b_far(c, k, v):
        return remote(
            send_b.at[c, far_slab(k) + v], recv_b.at[c, group + spot],
            sends.at[4], b_rsem.at[c], "expert", far_base + hub_lead(k) + v * hubs,
        )

    def sent(ref, sem, dev):
        remote(ref, ref, sem, sem, "expert", dev).wait_send()

    def s_raw(s, v=None):
        v = my_half if v is None else v
        return remote(
            sts.at[s], psts.at[s, v], sr_ssem.at[s], sr_rsem.at[s, v], "expert", far_hub
        )

    def s_own(s, k):
        return remote(
            send_s.at[s, near_spot(k)], recv_s.at[s, spot],
            s_ssem.at[s], s_rsem.at[s], "expert", near(k),
        )

    def s_far(s, k):
        return remote(
            send_q.at[s, near_spot(k)], recv_s.at[s, pl.ds(far_slab(0), 2)],
            q_ssem.at[s], s_rsem.at[s], "expert", near(k),
        )

    def s_in(s, count):
        return remote(
            recv_s.at[s, 0:count], recv_s.at[s, 0:count], s_ssem.at[s], s_rsem.at[s],
            "expert", near(1),
        )

    def tb_copy():
        return remote(rgb, rgp.at[my_half], tb_ssem.at[0], tb_rsem.at[my_half], "expert", far_hub)

    def tb_in(v):
        return remote(rgb, rgp.at[v], tb_ssem.at[0], tb_rsem.at[v], "expert", far_hub)

    def send_raw_a(c):
        abf[c] = adj[c].astype(bf)
        a_raw(c).start()

    def pack_own_a(s, c):
        pack(s, 0, lambda at, n: abf[c, :, at : at + n], dc, send_a.at[c])
        for k in range(1, group):
            a_own(c, k).start()
        recv_a[c, spot] = send_a[c, spot]

    def pack_far_a(s, c):
        for v in range(2):
            a_raw(c, v).wait_recv()
            pack(s, 1 + v, lambda at, n: araw[v, c, :, at : at + n], dc, send_f.at[c, :, v])
        for k in range(1, group):
            a_far(c, k).start()
        recv_a[c, pl.ds(far_slab(0), 2)] = send_f[c, spot]

    def pack_own_s(s):
        pack(s, 0, lambda at, n: sts[s, :, at : at + n], width, send_s.at[s])
        for k in range(1, group):
            s_own(s, k).start()
        recv_s[s, spot] = send_s[s, spot]

    def pack_far_s(s):
        for v in range(2):
            s_raw(s, v).wait_recv()
            pack(s, 1 + v, lambda at, n: psts[s, v, :, at : at + n], width, send_q.at[s, :, v])
        for k in range(1, group):
            s_far(s, k).start()
        recv_s[s, pl.ds(far_slab(0), 2)] = send_q[s, spot]

    def wait_slabs(copy_in):
        @pl.when(is_hub)
        def _():
            copy_in(group - 1 + 2 * (hubs - 1)).wait_recv()

        @pl.when(jnp.logical_not(is_hub))
        def _():
            copy_in(group - 1 + 2 * hubs).wait_recv()

    last = steps - 1
    late = lax.rem(t, 2) == 1
    early = lax.rem(t, 2) == 0

    def turn_over(source, target):
        def body(n, carry):
            at = pl.multiple_of(n * TURN, TURN)
            for m in range(0, source.shape[1], TURN):
                target[m : m + TURN, pl.ds(at, TURN)] = source[pl.ds(at, TURN), m : m + TURN].T
            return carry

        lax.fori_loop(0, source.shape[0] // TURN, body, 0)

    def turn_out():
        for copy in weights[CHUNKS:]:
            copy.wait()
        turn_over(wout, wout_t)

    def turn_in():
        for copy in weights[:CHUNKS]:
            copy.wait()
        turn_over(win, win_t)

    def send_all_raw_a():
        for c in range(CHUNKS):
            own_terminal[c].wait()
            send_raw_a(c)

    @pl.when(early)
    def _():
        send_all_raw_a()

    row = lax.broadcasted_iota(jnp.int32, (slots, slots), 0)
    col = lax.broadcasted_iota(jnp.int32, (slots, slots), 1)
    for u in tails:
        for j in range(fill):
            shift = 4 * (u - j)
            take = jnp.logical_and(col == row + shift, (row % SLAB) // 4 == j)
            give = jnp.logical_and(row == col + shift, (col % SLAB) // 4 == j)
            span = slice(j * slots, (j + 1) * slots)
            gather[u - fill, :, span] = jnp.where(take, 1.0, 0.0).astype(bf)
            scatter[u - fill, span, :] = jnp.where(give, 1.0, 0.0).astype(bf)

    wait_rg(last)
    tables(rgb, last, 0)
    tables(rgb, last, 3)

    @pl.when(early)
    def _():
        for c in range(CHUNKS):
            pack_own_a(last, c)

    for s in range(last):
        wait_rg(s)
    tb_copy().start()

    @pl.when(t != last)
    def _():
        for k in range(1, steps):
            st_copy(k).start()

    @pl.when(late)
    def _():
        turn_out()
        turn_in()
        send_all_raw_a()
        for c in range(CHUNKS):
            pack_own_a(last, c)

    wait_states(last)
    s_raw(last).start()
    pack_own_s(last)
    tb_copy().wait_send()

    @pl.when(is_hub)
    def _():
        for v in range(2):
            tb_in(v).wait_recv()
            tables(rgp.at[v], last, 1 + v)
        for c in range(CHUNKS):
            pack_far_a(last, c)
        pack_far_s(last)

    @pl.when(early)
    def _():
        turn_out()
        turn_in()

    def slope_rows(s):
        wait_slabs(lambda count: s_in(s, count))
        rows_in[...] = unpack(recv_s[s])

    def slope_part(c):
        part = pl.ds(c * fc, fc)
        pre = jnp.dot(rows_in[...], win[:, part], preferred_element_type=f32)
        slopes[:, part] = gelu_slope(pre)

    def out_remote(s, b, c):
        return remote(
            collect.at[s, c], out.at[0, block_rows(b), cols(c)],
            o_ssem.at[s, c], o_rsem.at[b, c], "tm", s,
        )

    def out_local(s, c):
        return pltpu.make_async_copy(
            collect.at[s, c], out.at[0, block_rows(t), cols(c)], l_sem.at[c]
        )

    def one_round(turn, carry):
        s = last - turn
        more = turn < last

        @pl.when(more)
        def _():
            wait_states(s - 1)
            s_raw(s - 1).start()
            tables(rgb, s - 1, 0)
            tables(rgb, s - 1, 3)

        @pl.when(jnp.logical_and(more, is_hub))
        def _():
            for v in range(2):
                tables(rgp.at[v], s - 1, 1 + v)

        @pl.when(turn > 0)
        def _():
            slope_rows(s)
            for c in range(CHUNKS):
                slope_part(c)

        for c in range(CHUNKS):
            wait_slabs(lambda count: a_in(c, count))
            term = jnp.dot(unpack(recv_a[c]), wout_t[cols(c), :], preferred_element_type=f32)
            if c == 0:
                back[...] = term
            else:
                back[...] += term

        @pl.when(turn == 0)
        def _():
            slope_rows(s)
            for c in range(CHUNKS):
                slope_part(c)

        hidden[...] = (back[...] * slopes[...]).astype(bf)
        for c in range(CHUNKS):
            answers = jnp.dot(hidden[...], win_t[:, cols(c)], preferred_element_type=f32)
            repack(answers, send_b.at[c])
            for k in range(hubs):
                for v in range(2):
                    b_far(c, k, v).start()
            for k in range(1, group):
                b_near(c, k).start()
            recv_b[c, spot] = send_b[c, spot]

        sent(abf, sends.at[0], far_hub)
        sent(send_a.at[:, 1:group], sends.at[1], near(1))

        @pl.when(is_hub)
        def _():
            sent(send_f.at[:, 1:group], sends.at[2], near(1))

        @pl.when(more)
        def _():
            pack_own_s(s - 1)

        @pl.when(jnp.logical_and(more, is_hub))
        def _():
            pack_far_s(s - 1)

        def finish(c):
            b_in(c).wait_recv()
            adj[c] = (
                adj[c] + combine(s, 0, recv_b[c, 0:group]) + combine(s, 1, recv_b[c, group:experts])
            )
            collect[s, c] = adj[c]

            @pl.when(more)
            def _():
                send_raw_a(c)
                pack_own_a(s - 1, c)

            @pl.when(s == t)
            def _():
                out_local(s, c).start()

            @pl.when(s != t)
            def _():
                out_remote(s, t, c).start()

        for c in range(CHUNKS):
            finish(c)

        @pl.when(jnp.logical_and(more, is_hub))
        def _():
            for c in range(CHUNKS):
                pack_far_a(s - 1, c)

        sent(send_b.at[:, 1:group], sends.at[3], near(1))
        sent(send_b.at[:, group:experts], sends.at[4], far_hub)

        return carry

    lax.fori_loop(0, steps, one_round, 0)

    for s in range(steps):
        s_raw(s).wait_send()
        sent(send_s.at[s, 1:group], s_ssem.at[s], near(1))

        @pl.when(is_hub)
        def _():
            sent(send_q.at[s, 1:group], q_ssem.at[s], near(1))

    for c in range(CHUNKS):
        out_local(t, c).wait()
    for k in range(1, steps):
        rg_copy(k).wait_send()
        st_copy(k).wait_send()
        b = tm_peer(k)
        for c in range(CHUNKS):
            out_remote(b, t, c).wait_send()
            out_remote(b, b, c).wait_recv()


def per_device(states, terminal, gates, routes, w_in, w_out):
    steps = lax.axis_size("tm")
    experts = lax.axis_size("expert")
    width = states.shape[2]
    ff = w_in.shape[2]
    top = routes.shape[2]
    tokens = states.shape[1]
    rows = tokens // steps
    cap = min(rows, (3 * MB * top + 2 * experts - 1) // (2 * experts))
    fill = -(-cap // 4)
    assert top == 2 and fill < QUARTERS and experts % 4 == 0
    group = experts // 2
    hubs = group // 2
    flat = group * SLAB
    slots = experts * SLAB
    dc = width // CHUNKS
    pc = dc * fill // QUARTERS
    ps = width * fill // QUARTERS
    kinds = 1 + QUARTERS - fill
    dma = pltpu.SemaphoreType.DMA
    bf = jnp.bfloat16
    f32 = jnp.float32
    vm = pltpu.VMEM
    return pl.pallas_call(
        functools.partial(kernel, steps, experts, fill, rows),
        out_shape=jax.ShapeDtypeStruct(states.shape, f32),
        in_specs=[pl.BlockSpec(memory_space=pl.ANY)] * 6,
        out_specs=pl.BlockSpec(memory_space=pl.ANY),
        scratch_shapes=[
            vm((2 * top, tokens), f32),
            vm((top, tokens), jnp.int32),
            vm((width, ff), bf),
            vm((ff, width), bf),
            vm((ff, width), bf),
            vm((width, ff), bf),
            vm((CHUNKS, rows, dc), f32),
            vm((CHUNKS, rows, dc), bf),
            vm((2, CHUNKS, rows, dc), bf),
            vm((steps, rows, width), bf),
            vm((steps, 2, rows, width), bf),
            vm((steps, 2 * top, tokens), f32),
            vm((2, steps, 2 * top, tokens), f32),
            vm((steps, 3, fill, flat, kinds * rows), bf),
            vm((steps, 2, fill, 2 * kinds * rows, flat), bf),
            vm((QUARTERS - fill, slots, fill * slots), bf),
            vm((QUARTERS - fill, fill * slots, slots), bf),
            vm((CHUNKS, group, SLAB, pc), bf),
            vm((CHUNKS, group, 2, SLAB, pc), bf),
            vm((CHUNKS, experts, SLAB, pc), bf),
            vm((CHUNKS, experts, SLAB, pc), bf),
            vm((CHUNKS, experts, SLAB, pc), bf),
            vm((steps, group, SLAB, ps), bf),
            vm((steps, group, 2, SLAB, ps), bf),
            vm((steps, experts, SLAB, ps), bf),
            vm((slots, ff), f32),
            vm((slots, ff), f32),
            vm((slots, ff), bf),
            vm((slots, width), bf),
            vm((steps, CHUNKS, rows, dc), f32),
            dma((2, CHUNKS)),
            dma((CHUNKS,)),
            dma((3,)),
            dma((CHUNKS,)),
            dma((steps - 1,)),
            dma((steps,)),
            dma((steps - 1,)),
            dma((steps,)),
            dma((1,)),
            dma((2,)),
            dma((5,)),
            dma((2, CHUNKS)),
            dma((CHUNKS,)),
            dma((CHUNKS,)),
            dma((steps,)),
            dma((steps, 2)),
            dma((steps,)),
            dma((steps,)),
            dma((steps,)),
            dma((steps, CHUNKS)),
            dma((steps, CHUNKS)),
        ],
        compiler_params=pltpu.CompilerParams(
            collective_id=0, has_side_effects=True, vmem_limit_bytes=60 * 1024 * 1024
        ),
    )(states, terminal, gates[0].T, routes[0].T, w_in, w_out)


def solution(mesh):
    placed = (
        P("tm", "expert", None),
        P("expert", None),
        P("tm", "expert", None),
        P("tm", "expert", None),
        P("expert", None, None),
        P("expert", None, None),
    )
    return jax.shard_map(
        per_device, mesh=mesh, in_specs=placed, out_specs=P("tm", "expert", None), check_vma=False
    )
```

```python
import functools

import jax
import jax.numpy as jnp
from jax import lax
from jax.experimental import pallas as pl
from jax.experimental.pallas import tpu as pltpu
from jax.sharding import PartitionSpec as P

MB = 32
CHUNKS = 2
TURN = 256
STEP_SIZE = 0.5
SLAB = 16
QUARTERS = 4


def gelu_slope(v):
    inside = 0.7978845608 * (v + 0.044715 * (v * v * v))
    t = jnp.tanh(inside)
    return 0.5 * (1.0 + t) + 0.5 * v * (1.0 - t * t) * 0.7978845608 * (
        1.0 + 3.0 * 0.044715 * v * v
    )


def kernel(
    steps, experts, fill, rows,
    states, terminal, gates, routes, w_in, w_out,
    out,
    rg, rt, win, wout, win_t, wout_t, adj, abf, araw, sts, psts, rgb, rgp, places, coefs, gather, scatter,
    send_a, send_f, recv_a, send_b, recv_b, send_s, send_q, recv_s,
    slopes, back, hidden, rows_in, collect,
    w_sem, t_sem, loc_sem, l_sem, rg_ssem, rg_rsem, st_ssem, st_rsem, tb_ssem, tb_rsem,
    sends, ar_rsem, a_rsem, b_rsem,
    sr_ssem, sr_rsem, s_ssem, q_ssem, s_rsem, o_ssem, o_rsem,
):
    t = lax.axis_index("tm")
    me = lax.axis_index("expert")
    width = win.shape[0]
    ff = win.shape[1]
    dc = width // CHUNKS
    fc = ff // CHUNKS
    group = experts // 2
    hubs = group // 2
    flat = group * SLAB
    slots = experts * SLAB
    tails = range(fill, QUARTERS)
    bf = jnp.bfloat16
    f32 = jnp.float32

    side = me // group
    base = side * group
    spot = me - base
    lead = lax.rem(me, hubs)
    far_base = (1 - side) * group
    is_hub = (spot // hubs) != side
    my_half = spot // hubs
    far_hub = far_base + side * hubs + lead

    def near_spot(k):
        return lax.rem(spot + k, group)

    def near(k):
        return base + near_spot(k)

    def far_owner(v):
        return far_base + lead + v * hubs

    def hub_lead(k):
        return lax.rem(lead + k, hubs)

    def near_hub(k):
        return base + (1 - side) * hubs + hub_lead(k)

    def cols(c):
        return pl.ds(c * dc, dc)

    def tm_peer(k):
        return lax.rem(t + k, steps)

    def remote(src, dst, ssem, rsem, axis, dev):
        return pltpu.make_async_remote_copy(
            src_ref=src, dst_ref=dst, send_sem=ssem, recv_sem=rsem,
            device_id={axis: dev}, device_id_type=pl.DeviceIdType.MESH,
        )

    def block_rows(b):
        return pl.ds(pl.multiple_of(b * rows, rows), rows)

    own_terminal = []
    for c in range(CHUNKS):
        copy = pltpu.make_async_copy(terminal.at[block_rows(t), cols(c)], adj.at[c], t_sem.at[c])
        copy.start()
        own_terminal.append(copy)
    own_states = pltpu.make_async_copy(states.at[0, block_rows(t)], sts.at[t], loc_sem.at[0])
    own_states.start()
    own_routes = pltpu.make_async_copy(routes, rt, loc_sem.at[1])
    own_routes.start()
    own_gates = pltpu.make_async_copy(gates, rg.at[2:4], loc_sem.at[2])
    own_gates.start()
    weights = []
    for c in range(CHUNKS):
        part = pl.ds(c * fc, fc)
        weights.append(pltpu.make_async_copy(w_in.at[0, :, part], win.at[:, part], w_sem.at[0, c]))
    for c in range(CHUNKS):
        weights.append(
            pltpu.make_async_copy(w_out.at[0, :, cols(c)], wout.at[:, cols(c)], w_sem.at[1, c])
        )
    for copy in weights[CHUNKS:] + weights[:CHUNKS]:
        copy.start()

    barrier = pltpu.get_barrier_semaphore()
    for k in range(1, experts):
        pl.semaphore_signal(
            barrier, inc=1, device_id={"expert": lax.rem(me + k, experts)},
            device_id_type=pl.DeviceIdType.MESH,
        )
    for k in range(1, steps):
        pl.semaphore_signal(
            barrier, inc=1, device_id={"tm": tm_peer(k)}, device_id_type=pl.DeviceIdType.MESH
        )
    own_routes.wait()
    own_gates.wait()
    rg[0:2] = rt[...].astype(f32)
    rgb[t] = rg[...]
    pl.semaphore_wait(barrier, experts + steps - 2)

    def rg_copy(k):
        return remote(rg, rgb.at[t], rg_ssem.at[k - 1], rg_rsem.at[t], "tm", tm_peer(k))

    def st_copy(k):
        b = tm_peer(k)
        return remote(
            states.at[0, block_rows(b)], sts.at[t], st_ssem.at[k - 1], st_rsem.at[t], "tm", b
        )

    def wait_rg(s):
        @pl.when(s != t)
        def _():
            remote(rg, rgb.at[s], rg_ssem.at[0], rg_rsem.at[s], "tm", s).wait_recv()

    def wait_states(s):
        @pl.when(s == t)
        def _():
            own_states.wait()

        @pl.when(s != t)
        def _():
            remote(
                states.at[0, block_rows(s)], sts.at[s], st_ssem.at[0], st_rsem.at[s], "tm", s
            ).wait_recv()

    for k in range(1, steps):
        rg_copy(k).start()

    @pl.when(t == steps - 1)
    def _():
        for k in range(1, steps):
            st_copy(k).start()

    lane = lax.broadcasted_iota(jnp.int32, (rows, flat), 1)
    near_expert = (lane // SLAB + base).astype(f32)
    far_expert = (lane // SLAB + far_base).astype(f32)
    place = lane % SLAB
    main_slot = jnp.where(place < 4 * fill, place, -1).astype(f32)

    def tail_slot(j, u):
        return jnp.where(place // 4 == u, 4 * j + place % 4, -1).astype(f32)

    earlier = (
        lax.broadcasted_iota(jnp.int32, (rows, rows), 1)
        < lax.broadcasted_iota(jnp.int32, (rows, rows), 0)
    ).astype(f32).astype(bf)
    tokens = rgb.shape[2]
    pick = lax.broadcasted_iota(jnp.int32, (rows, tokens), 1) == (
        t * rows + lax.broadcasted_iota(jnp.int32, (rows, tokens), 0)
    )

    def tables(source, s, blk):
        lane_expert = far_expert if blk == 3 else near_expert

        def column(n):
            return jnp.sum(jnp.where(pick, source[s, n : n + 1, :], 0.0), axis=1, keepdims=True)

        first = jnp.where(column(0) == lane_expert, 1.0, 0.0)
        second = jnp.where(column(1) == lane_expert, 1.0, 0.0)
        routed = first + second
        before = jnp.dot(earlier, routed.astype(bf), preferred_element_type=f32)
        weight = STEP_SIZE * (column(2) * first + column(3) * second)

        def pieces(slot):
            here = jnp.where(before == slot, 1.0, 0.0)
            scaled = weight * here
            high = scaled.astype(bf)
            low = (scaled - high.astype(f32)).astype(bf)
            return routed * here, [high, low]

        main, main_coefs = pieces(main_slot)
        for j in range(fill):
            chosen = [main]
            scales = list(main_coefs)
            for u in tails:
                tail, tail_coefs = pieces(tail_slot(j, u))
                chosen.append(tail)
                scales.extend(tail_coefs)
            if blk < 3:
                places[s, blk, j] = jnp.concatenate(chosen, axis=0).T.astype(bf)
            if blk % 3 == 0:
                coefs[s, blk // 3, j] = jnp.concatenate(scales, axis=0)

    def pack(s, blk, source, wide, target):
        qw = wide // QUARTERS
        for j in range(fill):
            stack = jnp.concatenate(
                [source(j * qw, qw)] + [source(u * qw, qw) for u in tails], axis=0
            )
            block = jnp.dot(places[s, blk, j], stack, preferred_element_type=f32)
            target[:, :, j * qw : (j + 1) * qw] = block.astype(bf).reshape(group, SLAB, qw)

    def unpack(piece):
        qw = piece.shape[2] // fill
        flatter = piece.reshape(slots, fill * qw)
        stack = jnp.concatenate([flatter[:, j * qw : (j + 1) * qw] for j in range(fill)], axis=0)
        ends = [
            jnp.dot(gather[u - fill], stack, preferred_element_type=f32).astype(bf) for u in tails
        ]
        return jnp.concatenate([flatter] + ends, axis=1)

    def repack(answers, target):
        qw = answers.shape[1] // QUARTERS
        moved = None
        for u in tails:
            low = answers[:, u * qw : (u + 1) * qw].astype(bf)
            term = jnp.dot(scatter[u - fill], low, preferred_element_type=f32)
            moved = term if moved is None else moved + term
        upper = lax.broadcasted_iota(jnp.int32, (slots, qw), 0) % SLAB < 4 * fill
        for j in range(fill):
            block = jnp.where(
                upper, answers[:, j * qw : (j + 1) * qw], moved[j * slots : (j + 1) * slots]
            )
            target[:, :, j * qw : (j + 1) * qw] = block.astype(bf).reshape(experts, SLAB, qw)

    def combine(s, blk, piece):
        qw = piece.shape[2] // fill
        flatter = piece.reshape(flat, fill * qw)
        mains = []
        ends = [None for _ in tails]
        for j in range(fill):
            got = jnp.dot(
                coefs[s, blk, j], flatter[:, j * qw : (j + 1) * qw], preferred_element_type=f32
            )
            mains.append(got[:rows] + got[rows : 2 * rows])
            for n in range(len(ends)):
                at = 2 * rows * (n + 1)
                term = got[at : at + rows] + got[at + rows : at + 2 * rows]
                ends[n] = term if ends[n] is None else ends[n] + term
        return jnp.concatenate(mains + ends, axis=1)

    def far_slab(k):
        return group + 2 * hub_lead(k)

    def a_raw(c, v=None):
        v = my_half if v is None else v
        return remote(abf.at[c], araw.at[v, c], sends.at[0], ar_rsem.at[v, c], "expert", far_hub)

    def a_own(c, k):
        return remote(
            send_a.at[c, near_spot(k)], recv_a.at[c, spot],
            sends.at[1], a_rsem.at[c], "expert", near(k),
        )

    def a_far(c, k, v):
        return remote(
            send_f.at[c, near_spot(k), v], recv_a.at[c, far_slab(0) + v],
            sends.at[2], a_rsem.at[c], "expert", near(k),
        )

    def a_in(c, count):
        return remote(
            send_b.at[c, 0:count], recv_a.at[c, 0:count], sends.at[1], a_rsem.at[c],
            "expert", near(1),
        )

    def b_near(c, k):
        return remote(
            send_b.at[c, near_spot(k)], recv_b.at[c, spot],
            sends.at[3], b_rsem.at[c], "expert", near(k),
        )

    def b_in(c):
        return remote(
            send_b.at[c, 1:experts], recv_b.at[c, 1:experts],
            sends.at[3], b_rsem.at[c], "expert", near(1),
        )

    def b_far(c, k, v):
        return remote(
            send_b.at[c, far_slab(k) + v], recv_b.at[c, group + spot],
            sends.at[4], b_rsem.at[c], "expert", far_base + hub_lead(k) + v * hubs,
        )

    def sent(ref, sem, dev):
        remote(ref, ref, sem, sem, "expert", dev).wait_send()

    def s_raw(s, v=None):
        v = my_half if v is None else v
        return remote(
            sts.at[s], psts.at[s, v], sr_ssem.at[s], sr_rsem.at[s, v], "expert", far_hub
        )

    def s_own(s, k):
        return remote(
            send_s.at[s, near_spot(k)], recv_s.at[s, spot],
            s_ssem.at[s], s_rsem.at[s], "expert", near(k),
        )

    def s_far(s, k):
        return remote(
            send_q.at[s, near_spot(k)], recv_s.at[s, pl.ds(far_slab(0), 2)],
            q_ssem.at[s], s_rsem.at[s], "expert", near(k),
        )

    def s_in(s, count):
        return remote(
            recv_s.at[s, 0:count], recv_s.at[s, 0:count], s_ssem.at[s], s_rsem.at[s],
            "expert", near(1),
        )

    def tb_copy():
        return remote(rgb, rgp.at[my_half], tb_ssem.at[0], tb_rsem.at[my_half], "expert", far_hub)

    def tb_in(v):
        return remote(rgb, rgp.at[v], tb_ssem.at[0], tb_rsem.at[v], "expert", far_hub)

    def send_raw_a(c):
        abf[c] = adj[c].astype(bf)
        a_raw(c).start()

    def pack_own_a(s, c):
        pack(s, 0, lambda at, n: abf[c, :, at : at + n], dc, send_a.at[c])
        for k in range(1, group):
            a_own(c, k).start()
        recv_a[c, spot] = send_a[c, spot]

    def pack_far_a(s, c):
        for v in range(2):
            a_raw(c, v).wait_recv()
            pack(s, 1 + v, lambda at, n: araw[v, c, :, at : at + n], dc, send_f.at[c, :, v])
            for k in range(1, group):
                a_far(c, k, v).start()
        recv_a[c, pl.ds(far_slab(0), 2)] = send_f[c, spot]

    def pack_own_s(s):
        pack(s, 0, lambda at, n: sts[s, :, at : at + n], width, send_s.at[s])
        for k in range(1, group):
            s_own(s, k).start()
        recv_s[s, spot] = send_s[s, spot]

    def pack_far_s(s):
        for v in range(2):
            s_raw(s, v).wait_recv()
            pack(s, 1 + v, lambda at, n: psts[s, v, :, at : at + n], width, send_q.at[s, :, v])
        for k in range(1, group):
            s_far(s, k).start()
        recv_s[s, pl.ds(far_slab(0), 2)] = send_q[s, spot]

    def wait_slabs(copy_in):
        @pl.when(is_hub)
        def _():
            copy_in(group - 1 + 2 * (hubs - 1)).wait_recv()

        @pl.when(jnp.logical_not(is_hub))
        def _():
            copy_in(group - 1 + 2 * hubs).wait_recv()

    last = steps - 1
    late = lax.rem(t, 2) == 1
    early = lax.rem(t, 2) == 0

    def turn_over(source, target):
        def body(n, carry):
            at = pl.multiple_of(n * TURN, TURN)
            for m in range(0, source.shape[1], TURN):
                target[m : m + TURN, pl.ds(at, TURN)] = source[pl.ds(at, TURN), m : m + TURN].T
            return carry

        lax.fori_loop(0, source.shape[0] // TURN, body, 0)

    def turn_out():
        for copy in weights[CHUNKS:]:
            copy.wait()
        turn_over(wout, wout_t)

    def turn_in():
        for copy in weights[:CHUNKS]:
            copy.wait()
        turn_over(win, win_t)

    def send_all_raw_a():
        for c in range(CHUNKS):
            own_terminal[c].wait()
            send_raw_a(c)

    @pl.when(early)
    def _():
        send_all_raw_a()

    row = lax.broadcasted_iota(jnp.int32, (slots, slots), 0)
    col = lax.broadcasted_iota(jnp.int32, (slots, slots), 1)
    for u in tails:
        for j in range(fill):
            shift = 4 * (u - j)
            take = jnp.logical_and(col == row + shift, (row % SLAB) // 4 == j)
            give = jnp.logical_and(row == col + shift, (col % SLAB) // 4 == j)
            span = slice(j * slots, (j + 1) * slots)
            gather[u - fill, :, span] = jnp.where(take, 1.0, 0.0).astype(bf)
            scatter[u - fill, span, :] = jnp.where(give, 1.0, 0.0).astype(bf)

    wait_rg(last)
    tables(rgb, last, 0)
    tables(rgb, last, 3)

    @pl.when(early)
    def _():
        for c in range(CHUNKS):
            pack_own_a(last, c)

    for s in range(last):
        wait_rg(s)
    tb_copy().start()

    @pl.when(t != last)
    def _():
        for k in range(1, steps):
            st_copy(k).start()

    @pl.when(late)
    def _():
        turn_out()
        turn_in()
        wait_states(last)
        s_raw(last).start()
        send_all_raw_a()
        for c in range(CHUNKS):
            pack_own_a(last, c)

    @pl.when(early)
    def _():
        wait_states(last)
        s_raw(last).start()

    pack_own_s(last)
    tb_copy().wait_send()

    @pl.when(is_hub)
    def _():
        for v in range(2):
            tb_in(v).wait_recv()
            tables(rgp.at[v], last, 1 + v)
        for c in range(CHUNKS):
            pack_far_a(last, c)
        pack_far_s(last)

    @pl.when(early)
    def _():
        turn_out()
        turn_in()

    def slope_rows(s):
        wait_slabs(lambda count: s_in(s, count))
        rows_in[...] = unpack(recv_s[s])

    def slope_part(c):
        part = pl.ds(c * fc, fc)
        pre = jnp.dot(rows_in[...], win[:, part], preferred_element_type=f32)
        slopes[:, part] = gelu_slope(pre)

    def out_remote(s, b, c):
        return remote(
            collect.at[s, c], out.at[0, block_rows(b), cols(c)],
            o_ssem.at[s, c], o_rsem.at[b, c], "tm", s,
        )

    def out_local(s, c):
        return pltpu.make_async_copy(
            collect.at[s, c], out.at[0, block_rows(t), cols(c)], l_sem.at[c]
        )

    def one_round(turn, carry):
        s = last - turn
        more = turn < last

        @pl.when(more)
        def _():
            wait_states(s - 1)
            s_raw(s - 1).start()
            tables(rgb, s - 1, 0)
            tables(rgb, s - 1, 3)

        @pl.when(jnp.logical_and(more, is_hub))
        def _():
            for v in range(2):
                tables(rgp.at[v], s - 1, 1 + v)

        @pl.when(turn > 0)
        def _():
            slope_rows(s)
            for c in range(CHUNKS):
                slope_part(c)

        for c in range(CHUNKS):
            wait_slabs(lambda count: a_in(c, count))
            term = jnp.dot(unpack(recv_a[c]), wout_t[cols(c), :], preferred_element_type=f32)
            if c == 0:
                back[...] = term
            else:
                back[...] += term

        @pl.when(turn == 0)
        def _():
            slope_rows(s)
            for c in range(CHUNKS):
                slope_part(c)

        hidden[...] = (back[...] * slopes[...]).astype(bf)
        for c in range(CHUNKS):
            answers = jnp.dot(hidden[...], win_t[:, cols(c)], preferred_element_type=f32)
            repack(answers, send_b.at[c])
            for k in range(hubs):
                for v in range(2):
                    b_far(c, k, v).start()
            for k in range(1, group):
                b_near(c, k).start()
            recv_b[c, spot] = send_b[c, spot]

        sent(abf, sends.at[0], far_hub)
        sent(send_a.at[:, 1:group], sends.at[1], near(1))

        @pl.when(is_hub)
        def _():
            sent(send_f.at[:, 1:group], sends.at[2], near(1))

        @pl.when(more)
        def _():
            pack_own_s(s - 1)

        @pl.when(jnp.logical_and(more, is_hub))
        def _():
            pack_far_s(s - 1)

        def finish(c):
            b_in(c).wait_recv()
            adj[c] = (
                adj[c] + combine(s, 0, recv_b[c, 0:group]) + combine(s, 1, recv_b[c, group:experts])
            )
            collect[s, c] = adj[c]

            @pl.when(more)
            def _():
                send_raw_a(c)
                pack_own_a(s - 1, c)

            @pl.when(s == t)
            def _():
                out_local(s, c).start()

            @pl.when(s != t)
            def _():
                out_remote(s, t, c).start()

        for c in range(CHUNKS):
            finish(c)

        @pl.when(jnp.logical_and(more, is_hub))
        def _():
            for c in range(CHUNKS):
                pack_far_a(s - 1, c)

        sent(send_b.at[:, 1:group], sends.at[3], near(1))
        sent(send_b.at[:, group:experts], sends.at[4], far_hub)

        return carry

    lax.fori_loop(0, steps, one_round, 0)

    for s in range(steps):
        s_raw(s).wait_send()
        sent(send_s.at[s, 1:group], s_ssem.at[s], near(1))

        @pl.when(is_hub)
        def _():
            sent(send_q.at[s, 1:group], q_ssem.at[s], near(1))

    for c in range(CHUNKS):
        out_local(t, c).wait()
    for k in range(1, steps):
        rg_copy(k).wait_send()
        st_copy(k).wait_send()
        b = tm_peer(k)
        for c in range(CHUNKS):
            out_remote(b, t, c).wait_send()
            out_remote(b, b, c).wait_recv()


def per_device(states, terminal, gates, routes, w_in, w_out):
    steps = lax.axis_size("tm")
    experts = lax.axis_size("expert")
    width = states.shape[2]
    ff = w_in.shape[2]
    top = routes.shape[2]
    tokens = states.shape[1]
    rows = tokens // steps
    cap = min(rows, (3 * MB * top + 2 * experts - 1) // (2 * experts))
    fill = -(-cap // 4)
    assert top == 2 and fill < QUARTERS and experts % 4 == 0
    group = experts // 2
    hubs = group // 2
    flat = group * SLAB
    slots = experts * SLAB
    dc = width // CHUNKS
    pc = dc * fill // QUARTERS
    ps = width * fill // QUARTERS
    kinds = 1 + QUARTERS - fill
    dma = pltpu.SemaphoreType.DMA
    bf = jnp.bfloat16
    f32 = jnp.float32
    vm = pltpu.VMEM
    return pl.pallas_call(
        functools.partial(kernel, steps, experts, fill, rows),
        out_shape=jax.ShapeDtypeStruct(states.shape, f32),
        in_specs=[pl.BlockSpec(memory_space=pl.ANY)] * 6,
        out_specs=pl.BlockSpec(memory_space=pl.ANY),
        scratch_shapes=[
            vm((2 * top, tokens), f32),
            vm((top, tokens), jnp.int32),
            vm((width, ff), bf),
            vm((ff, width), bf),
            vm((ff, width), bf),
            vm((width, ff), bf),
            vm((CHUNKS, rows, dc), f32),
            vm((CHUNKS, rows, dc), bf),
            vm((2, CHUNKS, rows, dc), bf),
            vm((steps, rows, width), bf),
            vm((steps, 2, rows, width), bf),
            vm((steps, 2 * top, tokens), f32),
            vm((2, steps, 2 * top, tokens), f32),
            vm((steps, 3, fill, flat, kinds * rows), bf),
            vm((steps, 2, fill, 2 * kinds * rows, flat), bf),
            vm((QUARTERS - fill, slots, fill * slots), bf),
            vm((QUARTERS - fill, fill * slots, slots), bf),
            vm((CHUNKS, group, SLAB, pc), bf),
            vm((CHUNKS, group, 2, SLAB, pc), bf),
            vm((CHUNKS, experts, SLAB, pc), bf),
            vm((CHUNKS, experts, SLAB, pc), bf),
            vm((CHUNKS, experts, SLAB, pc), bf),
            vm((steps, group, SLAB, ps), bf),
            vm((steps, group, 2, SLAB, ps), bf),
            vm((steps, experts, SLAB, ps), bf),
            vm((slots, ff), f32),
            vm((slots, ff), f32),
            vm((slots, ff), bf),
            vm((slots, width), bf),
            vm((steps, CHUNKS, rows, dc), f32),
            dma((2, CHUNKS)),
            dma((CHUNKS,)),
            dma((3,)),
            dma((CHUNKS,)),
            dma((steps - 1,)),
            dma((steps,)),
            dma((steps - 1,)),
            dma((steps,)),
            dma((1,)),
            dma((2,)),
            dma((5,)),
            dma((2, CHUNKS)),
            dma((CHUNKS,)),
            dma((CHUNKS,)),
            dma((steps,)),
            dma((steps, 2)),
            dma((steps,)),
            dma((steps,)),
            dma((steps,)),
            dma((steps, CHUNKS)),
            dma((steps, CHUNKS)),
        ],
        compiler_params=pltpu.CompilerParams(
            collective_id=0, has_side_effects=True, vmem_limit_bytes=60 * 1024 * 1024
        ),
    )(states, terminal, gates[0].T, routes[0].T, w_in, w_out)


def solution(mesh):
    placed = (
        P("tm", "expert", None),
        P("expert", None),
        P("tm", "expert", None),
        P("tm", "expert", None),
        P("expert", None, None),
        P("expert", None, None),
    )
    return jax.shard_map(
        per_device, mesh=mesh, in_specs=placed, out_specs=P("tm", "expert", None), check_vma=False
    )
```

```python
import functools

import jax
import jax.numpy as jnp
from jax import lax
from jax.experimental import pallas as pl
from jax.experimental.pallas import tpu as pltpu
from jax.sharding import PartitionSpec as P

MB = 32
CHUNKS = 2
TURN = 256
STEP_SIZE = 0.5
PARTS = 8
SLAB = 16
QUARTERS = 4


def gelu_slope(v):
    inside = 0.7978845608 * (v + 0.044715 * (v * v * v))
    t = jnp.tanh(inside)
    return 0.5 * (1.0 + t) + 0.5 * v * (1.0 - t * t) * 0.7978845608 * (
        1.0 + 3.0 * 0.044715 * v * v
    )


def kernel(
    steps, experts, fill, rows,
    states, terminal, gates, routes, w_in, w_out,
    out,
    rg, rt, win, wout, win_t, wout_t, adj, abf, araw, sts, psts, rgb, rgp, places, coefs, gather, scatter,
    send_a, send_f, recv_a, send_b, recv_b, send_s, send_q, recv_s,
    slopes, back, hidden, rows_in, collect,
    w_sem, t_sem, loc_sem, l_sem, rg_ssem, rg_rsem, st_ssem, st_rsem, tb_ssem, tb_rsem,
    sends, ar_rsem, a_rsem, b_rsem,
    sr_ssem, sr_rsem, s_ssem, q_ssem, s_rsem, o_ssem, o_rsem,
):
    t = lax.axis_index("tm")
    me = lax.axis_index("expert")
    width = win.shape[0]
    ff = win.shape[1]
    dc = width // CHUNKS
    fc = ff // CHUNKS
    group = experts // 2
    hubs = group // 2
    flat = group * SLAB
    slots = experts * SLAB
    tails = range(fill, QUARTERS)
    bf = jnp.bfloat16
    f32 = jnp.float32

    side = me // group
    base = side * group
    spot = me - base
    lead = lax.rem(me, hubs)
    far_base = (1 - side) * group
    is_hub = (spot // hubs) != side
    my_half = spot // hubs
    far_hub = far_base + side * hubs + lead

    def near_spot(k):
        return lax.rem(spot + k, group)

    def near(k):
        return base + near_spot(k)

    def far_owner(v):
        return far_base + lead + v * hubs

    def hub_lead(k):
        return lax.rem(lead + k, hubs)

    def near_hub(k):
        return base + (1 - side) * hubs + hub_lead(k)

    def cols(c):
        return pl.ds(c * dc, dc)

    def tm_peer(k):
        return lax.rem(t + k, steps)

    def remote(src, dst, ssem, rsem, axis, dev):
        return pltpu.make_async_remote_copy(
            src_ref=src, dst_ref=dst, send_sem=ssem, recv_sem=rsem,
            device_id={axis: dev}, device_id_type=pl.DeviceIdType.MESH,
        )

    def block_rows(b):
        return pl.ds(pl.multiple_of(b * rows, rows), rows)

    own_terminal = []
    for c in range(CHUNKS):
        copy = pltpu.make_async_copy(terminal.at[block_rows(t), cols(c)], adj.at[c], t_sem.at[c])
        copy.start()
        own_terminal.append(copy)
    own_states = pltpu.make_async_copy(states.at[0, block_rows(t)], sts.at[t], loc_sem.at[0])
    own_states.start()
    own_routes = pltpu.make_async_copy(routes, rt, loc_sem.at[1])
    own_routes.start()
    own_gates = pltpu.make_async_copy(gates, rg.at[2:4], loc_sem.at[2])
    own_gates.start()
    weights = []
    for c in range(CHUNKS):
        part = pl.ds(c * fc, fc)
        weights.append(pltpu.make_async_copy(w_in.at[0, :, part], win.at[:, part], w_sem.at[0, c]))
    for c in range(CHUNKS):
        weights.append(
            pltpu.make_async_copy(w_out.at[0, :, cols(c)], wout.at[:, cols(c)], w_sem.at[1, c])
        )
    for copy in weights[CHUNKS:] + weights[:CHUNKS]:
        copy.start()

    barrier = pltpu.get_barrier_semaphore()
    for k in range(1, experts):
        pl.semaphore_signal(
            barrier, inc=1, device_id={"expert": lax.rem(me + k, experts)},
            device_id_type=pl.DeviceIdType.MESH,
        )
    for k in range(1, steps):
        pl.semaphore_signal(
            barrier, inc=1, device_id={"tm": tm_peer(k)}, device_id_type=pl.DeviceIdType.MESH
        )
    own_routes.wait()
    own_gates.wait()
    rg[0:2] = rt[...].astype(f32)
    rgb[t] = rg[...]
    pl.semaphore_wait(barrier, experts + steps - 2)

    def rg_copy(k):
        return remote(rg, rgb.at[t], rg_ssem.at[k - 1], rg_rsem.at[t], "tm", tm_peer(k))

    def st_copy(k):
        b = tm_peer(k)
        return remote(
            states.at[0, block_rows(b)], sts.at[t], st_ssem.at[k - 1], st_rsem.at[t], "tm", b
        )

    def wait_rg(s):
        @pl.when(s != t)
        def _():
            remote(rg, rgb.at[s], rg_ssem.at[0], rg_rsem.at[s], "tm", s).wait_recv()

    def wait_states(s):
        @pl.when(s == t)
        def _():
            own_states.wait()

        @pl.when(s != t)
        def _():
            remote(
                states.at[0, block_rows(s)], sts.at[s], st_ssem.at[0], st_rsem.at[s], "tm", s
            ).wait_recv()

    for k in range(1, steps):
        rg_copy(k).start()

    @pl.when(t == steps - 1)
    def _():
        for k in range(1, steps):
            st_copy(k).start()

    lane = lax.broadcasted_iota(jnp.int32, (rows, flat), 1)
    near_expert = (lane // SLAB + base).astype(f32)
    far_expert = (lane // SLAB + far_base).astype(f32)
    place = lane % SLAB
    main_slot = jnp.where(place < 4 * fill, place, -1).astype(f32)

    def tail_slot(j, u):
        return jnp.where(place // 4 == u, 4 * j + place % 4, -1).astype(f32)

    earlier = (
        lax.broadcasted_iota(jnp.int32, (rows, rows), 1)
        < lax.broadcasted_iota(jnp.int32, (rows, rows), 0)
    ).astype(f32).astype(bf)
    tokens = rgb.shape[2]
    pick = lax.broadcasted_iota(jnp.int32, (rows, tokens), 1) == (
        t * rows + lax.broadcasted_iota(jnp.int32, (rows, tokens), 0)
    )

    def tables(source, s, blk):
        lane_expert = far_expert if blk == 3 else near_expert

        def column(n):
            return jnp.sum(jnp.where(pick, source[s, n : n + 1, :], 0.0), axis=1, keepdims=True)

        first = jnp.where(column(0) == lane_expert, 1.0, 0.0)
        second = jnp.where(column(1) == lane_expert, 1.0, 0.0)
        routed = first + second
        before = jnp.dot(earlier, routed.astype(bf), preferred_element_type=f32)
        weight = STEP_SIZE * (column(2) * first + column(3) * second)

        def pieces(slot):
            here = jnp.where(before == slot, 1.0, 0.0)
            scaled = weight * here
            high = scaled.astype(bf)
            low = (scaled - high.astype(f32)).astype(bf)
            return routed * here, [high, low]

        main, main_coefs = pieces(main_slot)
        for j in range(fill):
            chosen = [main]
            scales = list(main_coefs)
            for u in tails:
                tail, tail_coefs = pieces(tail_slot(j, u))
                chosen.append(tail)
                scales.extend(tail_coefs)
            if blk < 3:
                places[s, blk, j] = jnp.concatenate(chosen, axis=0).T.astype(bf)
            if blk % 3 == 0:
                coefs[s, blk // 3, j] = jnp.concatenate(scales, axis=0)

    def pack(s, blk, source, wide, target):
        qw = wide // QUARTERS
        for j in range(fill):
            stack = jnp.concatenate(
                [source(j * qw, qw)] + [source(u * qw, qw) for u in tails], axis=0
            )
            block = jnp.dot(places[s, blk, j], stack, preferred_element_type=f32)
            target[:, :, j * qw : (j + 1) * qw] = block.astype(bf).reshape(group, SLAB, qw)

    def unpack(piece):
        qw = piece.shape[2] // fill
        flatter = piece.reshape(slots, fill * qw)
        stack = jnp.concatenate([flatter[:, j * qw : (j + 1) * qw] for j in range(fill)], axis=0)
        ends = [
            jnp.dot(gather[u - fill], stack, preferred_element_type=f32).astype(bf) for u in tails
        ]
        return jnp.concatenate([flatter] + ends, axis=1)

    def repack(answers, target):
        qw = answers.shape[1] // QUARTERS
        moved = None
        for u in tails:
            low = answers[:, u * qw : (u + 1) * qw].astype(bf)
            term = jnp.dot(scatter[u - fill], low, preferred_element_type=f32)
            moved = term if moved is None else moved + term
        upper = lax.broadcasted_iota(jnp.int32, (slots, qw), 0) % SLAB < 4 * fill
        for j in range(fill):
            block = jnp.where(
                upper, answers[:, j * qw : (j + 1) * qw], moved[j * slots : (j + 1) * slots]
            )
            target[:, :, j * qw : (j + 1) * qw] = block.astype(bf).reshape(experts, SLAB, qw)

    def combine(s, blk, piece):
        qw = piece.shape[2] // fill
        flatter = piece.reshape(flat, fill * qw)
        mains = []
        ends = [None for _ in tails]
        for j in range(fill):
            got = jnp.dot(
                coefs[s, blk, j], flatter[:, j * qw : (j + 1) * qw], preferred_element_type=f32
            )
            mains.append(got[:rows] + got[rows : 2 * rows])
            for n in range(len(ends)):
                at = 2 * rows * (n + 1)
                term = got[at : at + rows] + got[at + rows : at + 2 * rows]
                ends[n] = term if ends[n] is None else ends[n] + term
        return jnp.concatenate(mains + ends, axis=1)

    def far_slab(k):
        return group + 2 * hub_lead(k)

    def a_raw(c, v=None):
        v = my_half if v is None else v
        return remote(abf.at[c], araw.at[v, c], sends.at[0], ar_rsem.at[v, c], "expert", far_hub)

    def a_own(c, k):
        return remote(
            send_a.at[c, near_spot(k)], recv_a.at[c, spot],
            sends.at[1], a_rsem.at[c], "expert", near(k),
        )

    def a_far(c, k, v):
        return remote(
            send_f.at[c, near_spot(k), v], recv_a.at[c, far_slab(0) + v],
            sends.at[2], a_rsem.at[c], "expert", near(k),
        )

    def a_in(c, count):
        return remote(
            send_b.at[c, 0:count], recv_a.at[c, 0:count], sends.at[1], a_rsem.at[c],
            "expert", near(1),
        )

    def b_near(c, k):
        return remote(
            send_b.at[c, near_spot(k)], recv_b.at[c, spot],
            sends.at[3], b_rsem.at[c], "expert", near(k),
        )

    def b_in(c):
        return remote(
            send_b.at[c, 1:experts], recv_b.at[c, 1:experts],
            sends.at[3], b_rsem.at[c], "expert", near(1),
        )

    def b_far(c, k, v):
        return remote(
            send_b.at[c, far_slab(k) + v], recv_b.at[c, group + spot],
            sends.at[4], b_rsem.at[c], "expert", far_base + hub_lead(k) + v * hubs,
        )

    def sent(ref, sem, dev):
        remote(ref, ref, sem, sem, "expert", dev).wait_send()

    def s_raw(s, v=None):
        v = my_half if v is None else v
        return remote(
            sts.at[s], psts.at[s, v], sr_ssem.at[s], sr_rsem.at[s, v], "expert", far_hub
        )

    def s_own(s, k):
        return remote(
            send_s.at[s, near_spot(k)], recv_s.at[s, spot],
            s_ssem.at[s], s_rsem.at[s], "expert", near(k),
        )

    def s_far(s, k):
        return remote(
            send_q.at[s, near_spot(k)], recv_s.at[s, pl.ds(far_slab(0), 2)],
            q_ssem.at[s], s_rsem.at[s], "expert", near(k),
        )

    def s_in(s, count):
        return remote(
            recv_s.at[s, 0:count], recv_s.at[s, 0:count], s_ssem.at[s], s_rsem.at[s],
            "expert", near(1),
        )

    def tb_copy():
        return remote(rgb, rgp.at[my_half], tb_ssem.at[0], tb_rsem.at[my_half], "expert", far_hub)

    def tb_in(v):
        return remote(rgb, rgp.at[v], tb_ssem.at[0], tb_rsem.at[v], "expert", far_hub)

    def send_raw_a(c):
        abf[c] = adj[c].astype(bf)
        a_raw(c).start()

    def pack_own_a(s, c):
        pack(s, 0, lambda at, n: abf[c, :, at : at + n], dc, send_a.at[c])
        for k in range(1, group):
            a_own(c, k).start()
        recv_a[c, spot] = send_a[c, spot]

    def pack_far_a(s, c):
        for v in range(2):
            a_raw(c, v).wait_recv()
            pack(s, 1 + v, lambda at, n: araw[v, c, :, at : at + n], dc, send_f.at[c, :, v])
            for k in range(1, group):
                a_far(c, k, v).start()
        recv_a[c, pl.ds(far_slab(0), 2)] = send_f[c, spot]

    def pack_own_s(s):
        pack(s, 0, lambda at, n: sts[s, :, at : at + n], width, send_s.at[s])
        for k in range(1, group):
            s_own(s, k).start()
        recv_s[s, spot] = send_s[s, spot]

    def pack_far_s(s):
        for v in range(2):
            s_raw(s, v).wait_recv()
            pack(s, 1 + v, lambda at, n: psts[s, v, :, at : at + n], width, send_q.at[s, :, v])
        for k in range(1, group):
            s_far(s, k).start()
        recv_s[s, pl.ds(far_slab(0), 2)] = send_q[s, spot]

    def wait_slabs(copy_in):
        @pl.when(is_hub)
        def _():
            copy_in(group - 1 + 2 * (hubs - 1)).wait_recv()

        @pl.when(jnp.logical_not(is_hub))
        def _():
            copy_in(group - 1 + 2 * hubs).wait_recv()

    last = steps - 1
    late = lax.rem(t, 2) == 1
    early = lax.rem(t, 2) == 0

    def turn_over(source, target):
        def body(n, carry):
            at = pl.multiple_of(n * TURN, TURN)
            for m in range(0, source.shape[1], TURN):
                target[m : m + TURN, pl.ds(at, TURN)] = source[pl.ds(at, TURN), m : m + TURN].T
            return carry

        lax.fori_loop(0, source.shape[0] // TURN, body, 0)

    def turn_out():
        for copy in weights[CHUNKS:]:
            copy.wait()
        turn_over(wout, wout_t)

    def turn_in():
        for copy in weights[:CHUNKS]:
            copy.wait()
        turn_over(win, win_t)

    def send_all_raw_a():
        for c in range(CHUNKS):
            own_terminal[c].wait()
            send_raw_a(c)

    @pl.when(early)
    def _():
        send_all_raw_a()

    row = lax.broadcasted_iota(jnp.int32, (slots, slots), 0)
    col = lax.broadcasted_iota(jnp.int32, (slots, slots), 1)
    for u in tails:
        for j in range(fill):
            shift = 4 * (u - j)
            take = jnp.logical_and(col == row + shift, (row % SLAB) // 4 == j)
            give = jnp.logical_and(row == col + shift, (col % SLAB) // 4 == j)
            span = slice(j * slots, (j + 1) * slots)
            gather[u - fill, :, span] = jnp.where(take, 1.0, 0.0).astype(bf)
            scatter[u - fill, span, :] = jnp.where(give, 1.0, 0.0).astype(bf)

    wait_rg(last)
    tables(rgb, last, 0)
    tables(rgb, last, 3)

    @pl.when(early)
    def _():
        for c in range(CHUNKS):
            pack_own_a(last, c)

    for s in range(last):
        wait_rg(s)
    tb_copy().start()

    @pl.when(t != last)
    def _():
        for k in range(1, steps):
            st_copy(k).start()

    @pl.when(late)
    def _():
        turn_out()
        turn_in()
        wait_states(last)
        s_raw(last).start()
        send_all_raw_a()
        for c in range(CHUNKS):
            pack_own_a(last, c)

    @pl.when(early)
    def _():
        wait_states(last)
        s_raw(last).start()

    pack_own_s(last)
    tb_copy().wait_send()

    @pl.when(is_hub)
    def _():
        for v in range(2):
            tb_in(v).wait_recv()
            tables(rgp.at[v], last, 1 + v)
        for c in range(CHUNKS):
            pack_far_a(last, c)
        pack_far_s(last)

    @pl.when(early)
    def _():
        turn_out()
        turn_in()

    def slope_rows(s):
        wait_slabs(lambda count: s_in(s, count))
        rows_in[...] = unpack(recv_s[s])

    def slope_part(c):
        part = pl.ds(c * fc, fc)
        pre = jnp.dot(rows_in[...], win[:, part], preferred_element_type=f32)
        slopes[:, part] = gelu_slope(pre)

    def out_remote(s, b, c):
        return remote(
            collect.at[s, c], out.at[0, block_rows(b), cols(c)],
            o_ssem.at[s, c], o_rsem.at[b, c], "tm", s,
        )

    def out_local(s, c):
        return pltpu.make_async_copy(
            collect.at[s, c], out.at[0, block_rows(t), cols(c)], l_sem.at[c]
        )

    def one_round(turn, carry):
        s = last - turn
        more = turn < last

        @pl.when(more)
        def _():
            wait_states(s - 1)
            s_raw(s - 1).start()
            tables(rgb, s - 1, 0)
            tables(rgb, s - 1, 3)

        @pl.when(jnp.logical_and(more, is_hub))
        def _():
            for v in range(2):
                tables(rgp.at[v], s - 1, 1 + v)

        @pl.when(turn > 0)
        def _():
            slope_rows(s)
            for c in range(CHUNKS):
                slope_part(c)

        for c in range(CHUNKS):
            wait_slabs(lambda count: a_in(c, count))
            term = jnp.dot(unpack(recv_a[c]), wout_t[cols(c), :], preferred_element_type=f32)
            if c == 0:
                back[...] = term
            else:
                back[...] += term

        @pl.when(turn == 0)
        def _():
            slope_rows(s)
            for c in range(CHUNKS):
                slope_part(c)

        hidden[...] = (back[...] * slopes[...]).astype(bf)
        for c in range(CHUNKS):
            answers = jnp.dot(hidden[...], win_t[:, cols(c)], preferred_element_type=f32)
            repack(answers, send_b.at[c])
            for k in range(hubs):
                for v in range(2):
                    b_far(c, k, v).start()
            for k in range(1, group):
                b_near(c, k).start()
            recv_b[c, spot] = send_b[c, spot]

        sent(abf, sends.at[0], far_hub)
        sent(send_a.at[:, 1:group], sends.at[1], near(1))

        @pl.when(is_hub)
        def _():
            sent(send_f.at[:, 1:group], sends.at[2], near(1))

        @pl.when(more)
        def _():
            pack_own_s(s - 1)

        @pl.when(jnp.logical_and(more, is_hub))
        def _():
            pack_far_s(s - 1)

        def finish(c):
            b_in(c).wait_recv()
            adj[c] = (
                adj[c] + combine(s, 0, recv_b[c, 0:group]) + combine(s, 1, recv_b[c, group:experts])
            )
            collect[s, c] = adj[c]

            @pl.when(more)
            def _():
                send_raw_a(c)
                pack_own_a(s - 1, c)

            @pl.when(s == t)
            def _():
                out_local(s, c).start()

            @pl.when(s != t)
            def _():
                out_remote(s, t, c).start()

        for c in range(CHUNKS):
            finish(c)

        @pl.when(jnp.logical_and(more, is_hub))
        def _():
            for c in range(CHUNKS):
                pack_far_a(s - 1, c)

        sent(send_b.at[:, 1:group], sends.at[3], near(1))
        sent(send_b.at[:, group:experts], sends.at[4], far_hub)

        return carry

    lax.fori_loop(0, steps, one_round, 0)

    for s in range(steps):
        s_raw(s).wait_send()
        sent(send_s.at[s, 1:group], s_ssem.at[s], near(1))

        @pl.when(is_hub)
        def _():
            sent(send_q.at[s, 1:group], q_ssem.at[s], near(1))

    for c in range(CHUNKS):
        out_local(t, c).wait()
    for k in range(1, steps):
        rg_copy(k).wait_send()
        st_copy(k).wait_send()
        b = tm_peer(k)
        for c in range(CHUNKS):
            out_remote(b, t, c).wait_send()
            out_remote(b, b, c).wait_recv()


def hand_over(found, out, held, in_sem, out_sem):
    part = found.shape[1] // PARTS
    spans = [pl.ds(n * part, part) for n in range(PARTS)]
    ins = [
        pltpu.make_async_copy(found.at[0, span], held.at[span], in_sem.at[n])
        for n, span in enumerate(spans)
    ]
    outs = [
        pltpu.make_async_copy(held.at[span], out.at[0, span], out_sem.at[n])
        for n, span in enumerate(spans)
    ]
    for copy in ins:
        copy.start()
    for n in range(PARTS):
        ins[n].wait()
        outs[n].start()
    for copy in outs:
        copy.wait()


def per_device(states, terminal, gates, routes, w_in, w_out):
    steps = lax.axis_size("tm")
    experts = lax.axis_size("expert")
    width = states.shape[2]
    ff = w_in.shape[2]
    top = routes.shape[2]
    tokens = states.shape[1]
    rows = tokens // steps
    cap = min(rows, (3 * MB * top + 2 * experts - 1) // (2 * experts))
    fill = -(-cap // 4)
    assert top == 2 and fill < QUARTERS and experts % 4 == 0
    group = experts // 2
    hubs = group // 2
    flat = group * SLAB
    slots = experts * SLAB
    dc = width // CHUNKS
    pc = dc * fill // QUARTERS
    ps = width * fill // QUARTERS
    kinds = 1 + QUARTERS - fill
    dma = pltpu.SemaphoreType.DMA
    bf = jnp.bfloat16
    f32 = jnp.float32
    vm = pltpu.VMEM
    found = pl.pallas_call(
        functools.partial(kernel, steps, experts, fill, rows),
        out_shape=jax.ShapeDtypeStruct(states.shape, f32),
        in_specs=[pl.BlockSpec(memory_space=pl.ANY)] * 6,
        out_specs=pl.BlockSpec(memory_space=pl.ANY),
        scratch_shapes=[
            vm((2 * top, tokens), f32),
            vm((top, tokens), jnp.int32),
            vm((width, ff), bf),
            vm((ff, width), bf),
            vm((ff, width), bf),
            vm((width, ff), bf),
            vm((CHUNKS, rows, dc), f32),
            vm((CHUNKS, rows, dc), bf),
            vm((2, CHUNKS, rows, dc), bf),
            vm((steps, rows, width), bf),
            vm((steps, 2, rows, width), bf),
            vm((steps, 2 * top, tokens), f32),
            vm((2, steps, 2 * top, tokens), f32),
            vm((steps, 3, fill, flat, kinds * rows), bf),
            vm((steps, 2, fill, 2 * kinds * rows, flat), bf),
            vm((QUARTERS - fill, slots, fill * slots), bf),
            vm((QUARTERS - fill, fill * slots, slots), bf),
            vm((CHUNKS, group, SLAB, pc), bf),
            vm((CHUNKS, group, 2, SLAB, pc), bf),
            vm((CHUNKS, experts, SLAB, pc), bf),
            vm((CHUNKS, experts, SLAB, pc), bf),
            vm((CHUNKS, experts, SLAB, pc), bf),
            vm((steps, group, SLAB, ps), bf),
            vm((steps, group, 2, SLAB, ps), bf),
            vm((steps, experts, SLAB, ps), bf),
            vm((slots, ff), f32),
            vm((slots, ff), f32),
            vm((slots, ff), bf),
            vm((slots, width), bf),
            vm((steps, CHUNKS, rows, dc), f32),
            dma((2, CHUNKS)),
            dma((CHUNKS,)),
            dma((3,)),
            dma((CHUNKS,)),
            dma((steps - 1,)),
            dma((steps,)),
            dma((steps - 1,)),
            dma((steps,)),
            dma((1,)),
            dma((2,)),
            dma((5,)),
            dma((2, CHUNKS)),
            dma((CHUNKS,)),
            dma((CHUNKS,)),
            dma((steps,)),
            dma((steps, 2)),
            dma((steps,)),
            dma((steps,)),
            dma((steps,)),
            dma((steps, CHUNKS)),
            dma((steps, CHUNKS)),
        ],
        compiler_params=pltpu.CompilerParams(
            collective_id=0, has_side_effects=True, vmem_limit_bytes=60 * 1024 * 1024
        ),
    )(states, terminal, gates[0].T, routes[0].T, w_in, w_out)
    return pl.pallas_call(
        hand_over,
        out_shape=jax.ShapeDtypeStruct(found.shape, f32),
        in_specs=[pl.BlockSpec(memory_space=pl.ANY)],
        out_specs=pl.BlockSpec(memory_space=pl.ANY),
        scratch_shapes=[vm(found.shape[1:], f32), dma((PARTS,)), dma((PARTS,))],
    )(found)


def solution(mesh):
    placed = (
        P("tm", "expert", None),
        P("expert", None),
        P("tm", "expert", None),
        P("tm", "expert", None),
        P("expert", None, None),
        P("expert", None, None),
    )
    return jax.shard_map(
        per_device, mesh=mesh, in_specs=placed, out_specs=P("tm", "expert", None), check_vma=False
    )
```

```python
import functools

import jax
import jax.numpy as jnp
from jax import lax
from jax.experimental import pallas as pl
from jax.experimental.pallas import tpu as pltpu
from jax.sharding import PartitionSpec as P

MB = 32
CHUNKS = 2
TURN = 256
STEP_SIZE = 0.5
PARTS = 8
SLAB = 16
QUARTERS = 4


def gelu_slope(v):
    inside = 0.7978845608 * (v + 0.044715 * (v * v * v))
    t = jnp.tanh(inside)
    return 0.5 * (1.0 + t) + 0.5 * v * (1.0 - t * t) * 0.7978845608 * (
        1.0 + 3.0 * 0.044715 * v * v
    )


def kernel(
    steps, experts, fill, rows,
    states, terminal, gates, routes, w_in, w_out,
    out,
    rg, rt, win, wout, win_t, wout_t, adj, abf, araw, sts, psts, rgb, rgp, places, coefs, gather, scatter,
    send_a, send_f, recv_a, send_b, recv_b, send_s, send_q, recv_s,
    slopes, back, hidden, rows_in, collect,
    w_sem, t_sem, loc_sem, l_sem, rg_ssem, rg_rsem, st_ssem, st_rsem, tb_ssem, tb_rsem,
    sends, ar_rsem, a_rsem, b_rsem, f_rsem,
    sr_ssem, sr_rsem, s_ssem, q_ssem, s_rsem, o_ssem, o_rsem,
):
    t = lax.axis_index("tm")
    me = lax.axis_index("expert")
    width = win.shape[0]
    ff = win.shape[1]
    dc = width // CHUNKS
    fc = ff // CHUNKS
    group = experts // 2
    hubs = group // 2
    flat = group * SLAB
    slots = experts * SLAB
    tails = range(fill, QUARTERS)
    bf = jnp.bfloat16
    f32 = jnp.float32

    side = me // group
    base = side * group
    spot = me - base
    lead = lax.rem(me, hubs)
    far_base = (1 - side) * group
    is_hub = (spot // hubs) != side
    my_half = spot // hubs
    far_hub = far_base + side * hubs + lead

    def near_spot(k):
        return lax.rem(spot + k, group)

    def near(k):
        return base + near_spot(k)

    def far_owner(v):
        return far_base + lead + v * hubs

    def hub_lead(k):
        return lax.rem(lead + k, hubs)

    def near_hub(k):
        return base + (1 - side) * hubs + hub_lead(k)

    def cols(c):
        return pl.ds(c * dc, dc)

    def tm_peer(k):
        return lax.rem(t + k, steps)

    def remote(src, dst, ssem, rsem, axis, dev):
        return pltpu.make_async_remote_copy(
            src_ref=src, dst_ref=dst, send_sem=ssem, recv_sem=rsem,
            device_id={axis: dev}, device_id_type=pl.DeviceIdType.MESH,
        )

    def block_rows(b):
        return pl.ds(pl.multiple_of(b * rows, rows), rows)

    own_terminal = []
    for c in range(CHUNKS):
        copy = pltpu.make_async_copy(terminal.at[block_rows(t), cols(c)], adj.at[c], t_sem.at[c])
        copy.start()
        own_terminal.append(copy)
    own_states = pltpu.make_async_copy(states.at[0, block_rows(t)], sts.at[t], loc_sem.at[0])
    own_states.start()
    own_routes = pltpu.make_async_copy(routes, rt, loc_sem.at[1])
    own_routes.start()
    own_gates = pltpu.make_async_copy(gates, rg.at[2:4], loc_sem.at[2])
    own_gates.start()
    weights = []
    for c in range(CHUNKS):
        part = pl.ds(c * fc, fc)
        weights.append(pltpu.make_async_copy(w_in.at[0, :, part], win.at[:, part], w_sem.at[0, c]))
    for c in range(CHUNKS):
        weights.append(
            pltpu.make_async_copy(w_out.at[0, :, cols(c)], wout.at[:, cols(c)], w_sem.at[1, c])
        )
    for copy in weights[CHUNKS:] + weights[:CHUNKS]:
        copy.start()

    barrier = pltpu.get_barrier_semaphore()
    for k in range(1, experts):
        pl.semaphore_signal(
            barrier, inc=1, device_id={"expert": lax.rem(me + k, experts)},
            device_id_type=pl.DeviceIdType.MESH,
        )
    for k in range(1, steps):
        pl.semaphore_signal(
            barrier, inc=1, device_id={"tm": tm_peer(k)}, device_id_type=pl.DeviceIdType.MESH
        )
    own_routes.wait()
    own_gates.wait()
    rg[0:2] = rt[...].astype(f32)
    rgb[t] = rg[...]
    pl.semaphore_wait(barrier, experts + steps - 2)

    def rg_copy(k):
        return remote(rg, rgb.at[t], rg_ssem.at[k - 1], rg_rsem.at[t], "tm", tm_peer(k))

    def st_copy(k):
        b = tm_peer(k)
        return remote(
            states.at[0, block_rows(b)], sts.at[t], st_ssem.at[k - 1], st_rsem.at[t], "tm", b
        )

    def wait_rg(s):
        @pl.when(s != t)
        def _():
            remote(rg, rgb.at[s], rg_ssem.at[0], rg_rsem.at[s], "tm", s).wait_recv()

    def wait_states(s):
        @pl.when(s == t)
        def _():
            own_states.wait()

        @pl.when(s != t)
        def _():
            remote(
                states.at[0, block_rows(s)], sts.at[s], st_ssem.at[0], st_rsem.at[s], "tm", s
            ).wait_recv()

    for k in range(1, steps):
        rg_copy(k).start()

    @pl.when(t == steps - 1)
    def _():
        for k in range(1, steps):
            st_copy(k).start()

    lane = lax.broadcasted_iota(jnp.int32, (rows, flat), 1)
    near_expert = (lane // SLAB + base).astype(f32)
    far_expert = (lane // SLAB + far_base).astype(f32)
    place = lane % SLAB
    main_slot = jnp.where(place < 4 * fill, place, -1).astype(f32)

    def tail_slot(j, u):
        return jnp.where(place // 4 == u, 4 * j + place % 4, -1).astype(f32)

    earlier = (
        lax.broadcasted_iota(jnp.int32, (rows, rows), 1)
        < lax.broadcasted_iota(jnp.int32, (rows, rows), 0)
    ).astype(f32).astype(bf)
    tokens = rgb.shape[2]
    pick = lax.broadcasted_iota(jnp.int32, (rows, tokens), 1) == (
        t * rows + lax.broadcasted_iota(jnp.int32, (rows, tokens), 0)
    )

    def tables(source, s, blk):
        lane_expert = far_expert if blk == 3 else near_expert

        def column(n):
            return jnp.sum(jnp.where(pick, source[s, n : n + 1, :], 0.0), axis=1, keepdims=True)

        first = jnp.where(column(0) == lane_expert, 1.0, 0.0)
        second = jnp.where(column(1) == lane_expert, 1.0, 0.0)
        routed = first + second
        before = jnp.dot(earlier, routed.astype(bf), preferred_element_type=f32)
        weight = STEP_SIZE * (column(2) * first + column(3) * second)

        def pieces(slot):
            here = jnp.where(before == slot, 1.0, 0.0)
            scaled = weight * here
            high = scaled.astype(bf)
            low = (scaled - high.astype(f32)).astype(bf)
            return routed * here, [high, low]

        main, main_coefs = pieces(main_slot)
        for j in range(fill):
            chosen = [main]
            scales = list(main_coefs)
            for u in tails:
                tail, tail_coefs = pieces(tail_slot(j, u))
                chosen.append(tail)
                scales.extend(tail_coefs)
            if blk < 3:
                places[s, blk, j] = jnp.concatenate(chosen, axis=0).T.astype(bf)
            if blk % 3 == 0:
                coefs[s, blk // 3, j] = jnp.concatenate(scales, axis=0)

    def pack(s, blk, source, wide, target):
        qw = wide // QUARTERS
        for j in range(fill):
            stack = jnp.concatenate(
                [source(j * qw, qw)] + [source(u * qw, qw) for u in tails], axis=0
            )
            block = jnp.dot(places[s, blk, j], stack, preferred_element_type=f32)
            target[:, :, j * qw : (j + 1) * qw] = block.astype(bf).reshape(group, SLAB, qw)

    def unpack(piece):
        qw = piece.shape[2] // fill
        flatter = piece.reshape(slots, fill * qw)
        stack = jnp.concatenate([flatter[:, j * qw : (j + 1) * qw] for j in range(fill)], axis=0)
        ends = [
            jnp.dot(gather[u - fill], stack, preferred_element_type=f32).astype(bf) for u in tails
        ]
        return jnp.concatenate([flatter] + ends, axis=1)

    def repack(answers, target):
        qw = answers.shape[1] // QUARTERS
        moved = None
        for u in tails:
            low = answers[:, u * qw : (u + 1) * qw].astype(bf)
            term = jnp.dot(scatter[u - fill], low, preferred_element_type=f32)
            moved = term if moved is None else moved + term
        upper = lax.broadcasted_iota(jnp.int32, (slots, qw), 0) % SLAB < 4 * fill
        for j in range(fill):
            block = jnp.where(
                upper, answers[:, j * qw : (j + 1) * qw], moved[j * slots : (j + 1) * slots]
            )
            target[:, :, j * qw : (j + 1) * qw] = block.astype(bf).reshape(experts, SLAB, qw)

    def combine(s, blk, piece):
        qw = piece.shape[2] // fill
        flatter = piece.reshape(flat, fill * qw)
        mains = []
        ends = [None for _ in tails]
        for j in range(fill):
            got = jnp.dot(
                coefs[s, blk, j], flatter[:, j * qw : (j + 1) * qw], preferred_element_type=f32
            )
            mains.append(got[:rows] + got[rows : 2 * rows])
            for n in range(len(ends)):
                at = 2 * rows * (n + 1)
                term = got[at : at + rows] + got[at + rows : at + 2 * rows]
                ends[n] = term if ends[n] is None else ends[n] + term
        return jnp.concatenate(mains + ends, axis=1)

    def far_slab(k):
        return group + 2 * hub_lead(k)

    def a_raw(c, v=None):
        v = my_half if v is None else v
        return remote(abf.at[c], araw.at[v, c], sends.at[0], ar_rsem.at[v, c], "expert", far_hub)

    def a_own(c, k):
        return remote(
            send_a.at[c, near_spot(k)], recv_a.at[c, spot],
            sends.at[1], a_rsem.at[c], "expert", near(k),
        )

    def a_far(c, k, v):
        return remote(
            send_f.at[c, near_spot(k), v], recv_a.at[c, far_slab(0) + v],
            sends.at[2], a_rsem.at[c], "expert", near(k),
        )

    def a_in(c, count):
        return remote(
            send_b.at[c, 0:count], recv_a.at[c, 0:count], sends.at[1], a_rsem.at[c],
            "expert", near(1),
        )

    def b_near(c, k):
        return remote(
            send_b.at[c, near_spot(k)], recv_b.at[c, spot],
            sends.at[3], b_rsem.at[c], "expert", near(k),
        )

    def b_near_in(c):
        return remote(
            send_b.at[c, 1:group], recv_b.at[c, 1:group],
            sends.at[3], b_rsem.at[c], "expert", near(1),
        )

    def b_far_in(c):
        return remote(
            send_b.at[c, group:experts], recv_b.at[c, group:experts],
            sends.at[4], f_rsem.at[c], "expert", far_hub,
        )

    def b_far(c, k, v):
        return remote(
            send_b.at[c, far_slab(k) + v], recv_b.at[c, group + spot],
            sends.at[4], f_rsem.at[c], "expert", far_base + hub_lead(k) + v * hubs,
        )

    def sent(ref, sem, dev):
        remote(ref, ref, sem, sem, "expert", dev).wait_send()

    def s_raw(s, v=None):
        v = my_half if v is None else v
        return remote(
            sts.at[s], psts.at[s, v], sr_ssem.at[s], sr_rsem.at[s, v], "expert", far_hub
        )

    def s_own(s, k):
        return remote(
            send_s.at[s, near_spot(k)], recv_s.at[s, spot],
            s_ssem.at[s], s_rsem.at[s], "expert", near(k),
        )

    def s_far(s, k):
        return remote(
            send_q.at[s, near_spot(k)], recv_s.at[s, pl.ds(far_slab(0), 2)],
            q_ssem.at[s], s_rsem.at[s], "expert", near(k),
        )

    def s_in(s, count):
        return remote(
            recv_s.at[s, 0:count], recv_s.at[s, 0:count], s_ssem.at[s], s_rsem.at[s],
            "expert", near(1),
        )

    def tb_copy():
        return remote(rgb, rgp.at[my_half], tb_ssem.at[0], tb_rsem.at[my_half], "expert", far_hub)

    def tb_in(v):
        return remote(rgb, rgp.at[v], tb_ssem.at[0], tb_rsem.at[v], "expert", far_hub)

    def send_raw_a(c):
        abf[c] = adj[c].astype(bf)
        a_raw(c).start()

    def pack_own_a(s, c):
        pack(s, 0, lambda at, n: abf[c, :, at : at + n], dc, send_a.at[c])
        for k in range(1, group):
            a_own(c, k).start()
        recv_a[c, spot] = send_a[c, spot]

    def pack_far_a(s, c):
        for v in range(2):
            a_raw(c, v).wait_recv()
            pack(s, 1 + v, lambda at, n: araw[v, c, :, at : at + n], dc, send_f.at[c, :, v])
            for k in range(1, group):
                a_far(c, k, v).start()
        recv_a[c, pl.ds(far_slab(0), 2)] = send_f[c, spot]

    def pack_own_s(s):
        pack(s, 0, lambda at, n: sts[s, :, at : at + n], width, send_s.at[s])
        for k in range(1, group):
            s_own(s, k).start()
        recv_s[s, spot] = send_s[s, spot]

    def pack_far_s(s):
        for v in range(2):
            s_raw(s, v).wait_recv()
            pack(s, 1 + v, lambda at, n: psts[s, v, :, at : at + n], width, send_q.at[s, :, v])
        for k in range(1, group):
            s_far(s, k).start()
        recv_s[s, pl.ds(far_slab(0), 2)] = send_q[s, spot]

    def wait_slabs(copy_in):
        @pl.when(is_hub)
        def _():
            copy_in(group - 1 + 2 * (hubs - 1)).wait_recv()

        @pl.when(jnp.logical_not(is_hub))
        def _():
            copy_in(group - 1 + 2 * hubs).wait_recv()

    last = steps - 1
    late = lax.rem(t, 2) == 1
    early = lax.rem(t, 2) == 0

    def turn_over(source, target):
        def body(n, carry):
            at = pl.multiple_of(n * TURN, TURN)
            for m in range(0, source.shape[1], TURN):
                target[m : m + TURN, pl.ds(at, TURN)] = source[pl.ds(at, TURN), m : m + TURN].T
            return carry

        lax.fori_loop(0, source.shape[0] // TURN, body, 0)

    def turn_out():
        for copy in weights[CHUNKS:]:
            copy.wait()
        turn_over(wout, wout_t)

    def turn_in():
        for copy in weights[:CHUNKS]:
            copy.wait()
        turn_over(win, win_t)

    def send_all_raw_a():
        for c in range(CHUNKS):
            own_terminal[c].wait()
            send_raw_a(c)

    @pl.when(early)
    def _():
        send_all_raw_a()

    row = lax.broadcasted_iota(jnp.int32, (slots, slots), 0)
    col = lax.broadcasted_iota(jnp.int32, (slots, slots), 1)
    for u in tails:
        for j in range(fill):
            shift = 4 * (u - j)
            take = jnp.logical_and(col == row + shift, (row % SLAB) // 4 == j)
            give = jnp.logical_and(row == col + shift, (col % SLAB) // 4 == j)
            span = slice(j * slots, (j + 1) * slots)
            gather[u - fill, :, span] = jnp.where(take, 1.0, 0.0).astype(bf)
            scatter[u - fill, span, :] = jnp.where(give, 1.0, 0.0).astype(bf)

    wait_rg(last)
    tables(rgb, last, 0)
    tables(rgb, last, 3)

    @pl.when(early)
    def _():
        for c in range(CHUNKS):
            pack_own_a(last, c)

    for s in range(last):
        wait_rg(s)
    tb_copy().start()

    @pl.when(t != last)
    def _():
        for k in range(1, steps):
            st_copy(k).start()

    @pl.when(late)
    def _():
        turn_out()
        turn_in()
        wait_states(last)
        s_raw(last).start()
        send_all_raw_a()
        for c in range(CHUNKS):
            pack_own_a(last, c)

    @pl.when(early)
    def _():
        wait_states(last)
        s_raw(last).start()

    pack_own_s(last)
    tb_copy().wait_send()

    @pl.when(is_hub)
    def _():
        for v in range(2):
            tb_in(v).wait_recv()
            tables(rgp.at[v], last, 1 + v)
        for c in range(CHUNKS):
            pack_far_a(last, c)
        pack_far_s(last)

    @pl.when(early)
    def _():
        turn_out()
        turn_in()

    def slope_rows(s):
        wait_slabs(lambda count: s_in(s, count))
        rows_in[...] = unpack(recv_s[s])

    def slope_part(c):
        part = pl.ds(c * fc, fc)
        pre = jnp.dot(rows_in[...], win[:, part], preferred_element_type=f32)
        slopes[:, part] = gelu_slope(pre)

    def out_remote(s, b, c):
        return remote(
            collect.at[s, c], out.at[0, block_rows(b), cols(c)],
            o_ssem.at[s, c], o_rsem.at[b, c], "tm", s,
        )

    def out_local(s, c):
        return pltpu.make_async_copy(
            collect.at[s, c], out.at[0, block_rows(t), cols(c)], l_sem.at[c]
        )

    def one_round(turn, carry):
        s = last - turn
        more = turn < last

        @pl.when(more)
        def _():
            wait_states(s - 1)
            s_raw(s - 1).start()
            tables(rgb, s - 1, 0)
            tables(rgb, s - 1, 3)

        @pl.when(jnp.logical_and(more, is_hub))
        def _():
            for v in range(2):
                tables(rgp.at[v], s - 1, 1 + v)

        @pl.when(turn > 0)
        def _():
            slope_rows(s)
            for c in range(CHUNKS):
                slope_part(c)

        for c in range(CHUNKS):
            wait_slabs(lambda count: a_in(c, count))
            term = jnp.dot(unpack(recv_a[c]), wout_t[cols(c), :], preferred_element_type=f32)
            if c == 0:
                back[...] = term
            else:
                back[...] += term

        @pl.when(turn == 0)
        def _():
            slope_rows(s)
            for c in range(CHUNKS):
                slope_part(c)

        hidden[...] = (back[...] * slopes[...]).astype(bf)
        for c in range(CHUNKS):
            answers = jnp.dot(hidden[...], win_t[:, cols(c)], preferred_element_type=f32)
            repack(answers, send_b.at[c])
            for k in range(hubs):
                for v in range(2):
                    b_far(c, k, v).start()
            for k in range(1, group):
                b_near(c, k).start()
            recv_b[c, spot] = send_b[c, spot]

        sent(abf, sends.at[0], far_hub)
        sent(send_a.at[:, 1:group], sends.at[1], near(1))

        @pl.when(is_hub)
        def _():
            sent(send_f.at[:, 1:group], sends.at[2], near(1))

        @pl.when(more)
        def _():
            pack_own_s(s - 1)

        @pl.when(jnp.logical_and(more, is_hub))
        def _():
            pack_far_s(s - 1)

        def finish(c):
            b_near_in(c).wait_recv()
            mine = adj[c] + combine(s, 0, recv_b[c, 0:group])
            b_far_in(c).wait_recv()
            adj[c] = mine + combine(s, 1, recv_b[c, group:experts])
            collect[s, c] = adj[c]

            @pl.when(more)
            def _():
                send_raw_a(c)
                pack_own_a(s - 1, c)

            @pl.when(s == t)
            def _():
                out_local(s, c).start()

            @pl.when(s != t)
            def _():
                out_remote(s, t, c).start()

        for c in range(CHUNKS):
            finish(c)

        @pl.when(jnp.logical_and(more, is_hub))
        def _():
            for c in range(CHUNKS):
                pack_far_a(s - 1, c)

        sent(send_b.at[:, 1:group], sends.at[3], near(1))
        sent(send_b.at[:, group:experts], sends.at[4], far_hub)

        return carry

    lax.fori_loop(0, steps, one_round, 0)

    for s in range(steps):
        s_raw(s).wait_send()
        sent(send_s.at[s, 1:group], s_ssem.at[s], near(1))

        @pl.when(is_hub)
        def _():
            sent(send_q.at[s, 1:group], q_ssem.at[s], near(1))

    for c in range(CHUNKS):
        out_local(t, c).wait()
    for k in range(1, steps):
        rg_copy(k).wait_send()
        st_copy(k).wait_send()
        b = tm_peer(k)
        for c in range(CHUNKS):
            out_remote(b, t, c).wait_send()
            out_remote(b, b, c).wait_recv()


def hand_over(found, out, held, in_sem, out_sem):
    part = found.shape[1] // PARTS
    spans = [pl.ds(n * part, part) for n in range(PARTS)]
    ins = [
        pltpu.make_async_copy(found.at[0, span], held.at[span], in_sem.at[n])
        for n, span in enumerate(spans)
    ]
    outs = [
        pltpu.make_async_copy(held.at[span], out.at[0, span], out_sem.at[n])
        for n, span in enumerate(spans)
    ]
    for copy in ins:
        copy.start()
    for n in range(PARTS):
        ins[n].wait()
        outs[n].start()
    for copy in outs:
        copy.wait()


def per_device(states, terminal, gates, routes, w_in, w_out):
    steps = lax.axis_size("tm")
    experts = lax.axis_size("expert")
    width = states.shape[2]
    ff = w_in.shape[2]
    top = routes.shape[2]
    tokens = states.shape[1]
    rows = tokens // steps
    cap = min(rows, (3 * MB * top + 2 * experts - 1) // (2 * experts))
    fill = -(-cap // 4)
    assert top == 2 and fill < QUARTERS and experts % 4 == 0
    group = experts // 2
    hubs = group // 2
    flat = group * SLAB
    slots = experts * SLAB
    dc = width // CHUNKS
    pc = dc * fill // QUARTERS
    ps = width * fill // QUARTERS
    kinds = 1 + QUARTERS - fill
    dma = pltpu.SemaphoreType.DMA
    bf = jnp.bfloat16
    f32 = jnp.float32
    vm = pltpu.VMEM
    found = pl.pallas_call(
        functools.partial(kernel, steps, experts, fill, rows),
        out_shape=jax.ShapeDtypeStruct(states.shape, f32),
        in_specs=[pl.BlockSpec(memory_space=pl.ANY)] * 6,
        out_specs=pl.BlockSpec(memory_space=pl.ANY),
        scratch_shapes=[
            vm((2 * top, tokens), f32),
            vm((top, tokens), jnp.int32),
            vm((width, ff), bf),
            vm((ff, width), bf),
            vm((ff, width), bf),
            vm((width, ff), bf),
            vm((CHUNKS, rows, dc), f32),
            vm((CHUNKS, rows, dc), bf),
            vm((2, CHUNKS, rows, dc), bf),
            vm((steps, rows, width), bf),
            vm((steps, 2, rows, width), bf),
            vm((steps, 2 * top, tokens), f32),
            vm((2, steps, 2 * top, tokens), f32),
            vm((steps, 3, fill, flat, kinds * rows), bf),
            vm((steps, 2, fill, 2 * kinds * rows, flat), bf),
            vm((QUARTERS - fill, slots, fill * slots), bf),
            vm((QUARTERS - fill, fill * slots, slots), bf),
            vm((CHUNKS, group, SLAB, pc), bf),
            vm((CHUNKS, group, 2, SLAB, pc), bf),
            vm((CHUNKS, experts, SLAB, pc), bf),
            vm((CHUNKS, experts, SLAB, pc), bf),
            vm((CHUNKS, experts, SLAB, pc), bf),
            vm((steps, group, SLAB, ps), bf),
            vm((steps, group, 2, SLAB, ps), bf),
            vm((steps, experts, SLAB, ps), bf),
            vm((slots, ff), f32),
            vm((slots, ff), f32),
            vm((slots, ff), bf),
            vm((slots, width), bf),
            vm((steps, CHUNKS, rows, dc), f32),
            dma((2, CHUNKS)),
            dma((CHUNKS,)),
            dma((3,)),
            dma((CHUNKS,)),
            dma((steps - 1,)),
            dma((steps,)),
            dma((steps - 1,)),
            dma((steps,)),
            dma((1,)),
            dma((2,)),
            dma((5,)),
            dma((2, CHUNKS)),
            dma((CHUNKS,)),
            dma((CHUNKS,)),
            dma((CHUNKS,)),
            dma((steps,)),
            dma((steps, 2)),
            dma((steps,)),
            dma((steps,)),
            dma((steps,)),
            dma((steps, CHUNKS)),
            dma((steps, CHUNKS)),
        ],
        compiler_params=pltpu.CompilerParams(
            collective_id=0, has_side_effects=True, vmem_limit_bytes=60 * 1024 * 1024
        ),
    )(states, terminal, gates[0].T, routes[0].T, w_in, w_out)
    return pl.pallas_call(
        hand_over,
        out_shape=jax.ShapeDtypeStruct(found.shape, f32),
        in_specs=[pl.BlockSpec(memory_space=pl.ANY)],
        out_specs=pl.BlockSpec(memory_space=pl.ANY),
        scratch_shapes=[vm(found.shape[1:], f32), dma((PARTS,)), dma((PARTS,))],
    )(found)


def solution(mesh):
    placed = (
        P("tm", "expert", None),
        P("expert", None),
        P("tm", "expert", None),
        P("tm", "expert", None),
        P("expert", None, None),
        P("expert", None, None),
    )
    return jax.shard_map(
        per_device, mesh=mesh, in_specs=placed, out_specs=P("tm", "expert", None), check_vma=False
    )
```
